32 devices in a mesh: blocks: 8 (over y, x, core), slab: 4 (over z).
Axes of the slice: x: 2, y: 2, z: 4, core: 2. Of those that a mesh axis runs over, the one named last changes fastest.
Arguments:
- populations: float32 [19, 4, 8, 4096], P(None, 'slab', 'blocks'), may hold values from -6 to 6
- w_in: bfloat16 [512, 19], replicated, may hold values from -1.25 to 1.25
- w_mid: bfloat16 [1, 512, 512], replicated, may hold values from -0.25 to 0.25
- w_out: bfloat16 [19, 512], replicated, may hold values from -0.25 to 0.25
- cotangent: float32 [19, 4, 8, 4096], P(None, 'slab', 'blocks'), may hold values from -6 to 6
- face_source: int32 [8, 4], replicated, may hold values from 0 to 7, as said below
- face_level: int32 [4, 8, 6], P('slab', 'blocks'), may hold values 0 or 1
- face_quadrant: int32 [4, 8, 6], P('slab', 'blocks'), may hold values from 0 to 3
Outputs:
- final: float32 [19, 4, 8, 4096], P(None, 'slab', 'blocks')
- grad_pops: float32 [19, 4, 8, 4096], P(None, 'slab', 'blocks')
- grad_in: float32 [512, 19], replicated
- grad_mid: float32 [1, 512, 512], replicated
- grad_out: float32 [19, 512], replicated
The draws below stay inside these ranges and needn't reach their ends.
Inputs may be any that keep to these rules, and one draw needn't show every extreme that they name: face_source is symmetric: face_source[face_source[b, f], f xor 1] = b. The +y and -y neighbours of block b are the same block, b xor 1. Every neighbour's index differs from the block's by at most 3 modulo 8, never by 0, and that distance is reached.
All inputs are finite; a program needn't handle non-finite values. No bound on the sum of `face_level` on one device may be relied on, other than what follows from the above.
Results may differ from the reference program's by a relative error of at most 0.0088.
Values sent between devices are 32-bit elements; how exact they have to be, the bound alone decides.
A program may use at most 128 MiB of HBM per device.

```python
from functools import partial
import jax
import jax.numpy as jnp
from jax import lax

Q = 19
HID = 512
MIDS = 1
S = 16
STEPS = 2
CELLS = 4096
GX = 4
CELLS_ALL = 131072
N_BLOCKS = 8
N_SLAB = 4


def placement_tables(key):
    flips = jax.random.randint(jax.random.fold_in(key, 7), (GX,), 0, 2).astype(jnp.int32)
    anchor = jax.random.randint(jax.random.fold_in(key, 11), (), 0, GX).astype(jnp.int32)
    mirror = jax.random.randint(jax.random.fold_in(key, 13), (), 0, 2).astype(jnp.int32)
    follow = (anchor + 1) % GX
    flips = flips.at[follow].set(1 - flips[anchor])
    location = jnp.arange(GX * 2, dtype=jnp.int32)
    column = location // 2
    stored = location % 2
    parity = jnp.bitwise_xor(stored, flips[column])
    next_column = (column + 1) % GX
    prior_column = (column + GX - 1) % GX
    forward_x = next_column * 2 + jnp.bitwise_xor(parity, flips[next_column])
    backward_x = prior_column * 2 + jnp.bitwise_xor(parity, flips[prior_column])
    plus_x = jnp.where(mirror == 1, backward_x, forward_x)
    minus_x = jnp.where(mirror == 1, forward_x, backward_x)
    other_y = column * 2 + (1 - stored)
    return jnp.stack([plus_x, minus_x, other_y, other_y], axis=1).astype(jnp.int32)


def draw_face_source(key, part):
    return placement_tables(key)


def with_ends(array, key, low, high):
    spot = [jax.random.randint(jax.random.fold_in(key, axis), (), 0, length) for axis, length in enumerate(array.shape)]
    longest = array.shape.index(max(array.shape))
    beside = spot[:longest] + [(spot[longest] + 1) % array.shape[longest]] + spot[longest + 1:]
    return array.at[tuple(spot)].set(low).at[tuple(beside)].set(high)


def level_of(stream_key, dims, shards, low, high):
    def one(dim, shards_of):
        heights = jax.random.uniform(jax.random.fold_in(jax.random.fold_in(stream_key, 6), dim), (shards_of,), jnp.float32, low / len(shards), high / len(shards))
        return jnp.repeat(jnp.exp(heights), dims[dim] // shards_of).reshape((-1,) + (1,) * (len(dims) - dim - 1))

    level = one(*shards[0])
    for cut in shards[1:]:
        level = level * one(*cut)
    return level


def centred(rng, extent, spread, most, split=(), kind=jnp.bfloat16):
    drawn = jax.random.normal(rng, extent, jnp.float32) * spread
    if len(split) > 0:
        drawn = level_of(rng, extent, split, -0.22, 0.18) * drawn
    return jnp.clip(drawn, min=-most, max=most).astype(kind)


def setup_inputs(seed: int = 0) -> dict:
    key_list = jax.random.split(jax.random.key(seed), 9)
    populations = centred(key_list[0], (Q, N_SLAB, N_BLOCKS, CELLS), 1.0, 6.0, ((1, 4), (2, 8)), jnp.float32)
    w_in = centred(key_list[1], (HID, Q), Q ** -0.5, 1.25)
    w_mid = centred(key_list[2], (MIDS, HID, HID), HID ** -0.5, 0.25)
    w_out = centred(key_list[3], (Q, HID), HID ** -0.5, 0.25)
    cotangent = centred(key_list[4], (Q, N_SLAB, N_BLOCKS, CELLS), 1.0, 6.0, ((1, 4), (2, 8)), jnp.float32)
    face_source = draw_face_source(jax.random.fold_in(key_list[8], 71), 0)
    face_level = with_ends((jax.random.randint(key_list[6], (N_SLAB, N_BLOCKS, 6), 0, 2) < 1).astype(jnp.int32), jax.random.fold_in(key_list[6], 1), 0, 1)
    face_quadrant = with_ends(jax.random.randint(key_list[7], (N_SLAB, N_BLOCKS, 6), 0, 4), jax.random.fold_in(key_list[7], 1), 0, 3).astype(jnp.int32)
    return {"populations": populations, "w_in": w_in, "w_mid": w_mid, "w_out": w_out, "cotangent": cotangent, "face_source": face_source, "face_level": face_level, "face_quadrant": face_quadrant}


VELOCITIES = [(0, 0, 0), (1, 0, 0), (-1, 0, 0), (0, 1, 0), (0, -1, 0), (0, 0, 1), (0, 0, -1), (1, 1, 0), (-1, -1, 0), (1, -1, 0), (-1, 1, 0), (1, 0, 1), (-1, 0, -1), (1, 0, -1), (-1, 0, 1), (0, 1, 1), (0, -1, -1), (0, 1, -1), (0, -1, 1)]
OPPOSITE = [0, 2, 1, 4, 3, 6, 5, 8, 7, 10, 9, 12, 11, 14, 13, 16, 15, 18, 17]

def face_members(face_id):
    along = face_id // 2
    sign_value = 1 if face_id % 2 == 0 else -1
    return [which for which in range(19) if VELOCITIES[which][along] == sign_value]

def face_layers(collided, block_side):
    cube_view = collided.reshape(collided.shape[0], block_side, block_side, block_side)
    sheets = []
    for face_id in range(6):
        along = face_id // 2
        layer_index = block_side - 1 if face_id % 2 == 0 else 0
        members = jnp.stack([cube_view[which] for which in face_members(face_id)])
        layer_sheet = lax.index_in_dim(members, layer_index, along + 1, keepdims=False)
        sheets.append(layer_sheet.reshape(5, block_side * block_side))
    return jnp.stack(sheets)

def refine_sheet(layer_sheet, levels, quadrant, block_side):
    square = layer_sheet.reshape(5, block_side, block_side)
    half_side = block_side // 2
    row_start = (quadrant // 2 * half_side).astype(jnp.int32)
    col_start = (quadrant % 2 * half_side).astype(jnp.int32)
    corner_part = lax.dynamic_slice(square, (jnp.zeros((), jnp.int32), row_start, col_start), (5, half_side, half_side))
    enlarged = jnp.repeat(jnp.repeat(corner_part, 2, axis=1), 2, axis=2)
    return jnp.where(levels == 1, enlarged, square).reshape(5, block_side * block_side)

def stream_block(collided, ghosts, block_side):
    cube_view = collided.reshape(collided.shape[0], block_side, block_side, block_side)
    shape3 = (block_side, block_side, block_side)
    coords = [lax.broadcasted_iota(jnp.int32, shape3, along) for along in range(3)]
    results = []
    for which in range(19):
        vector = VELOCITIES[which]
        shifted = jnp.roll(cube_view[which], shift=vector, axis=(0, 1, 2))
        crossed = jnp.zeros(shape3, jnp.int32)
        ghost_sum = jnp.zeros(shape3, jnp.float32)
        for along in range(3):
            if vector[along] != 0:
                leaving = coords[along] == (0 if vector[along] == 1 else block_side - 1)
                face_id = 2 * along + (0 if vector[along] == -1 else 1)
                position = face_members(face_id ^ 1).index(which)
                others = [other for other in range(3) if other != along]
                square = ghosts[face_id, position].reshape(block_side, block_side)
                square = jnp.roll(square, shift=(vector[others[0]], vector[others[1]]), axis=(0, 1))
                volume = jnp.expand_dims(square, along)
                ghost_sum = ghost_sum + jnp.where(leaving, volume, jnp.float32(0.0))
                crossed = crossed + leaving.astype(jnp.int32)
        chosen = jnp.where(crossed == 0, shifted, jnp.where(crossed == 1, ghost_sum, cube_view[OPPOSITE[which]]))
        results.append(chosen.reshape(-1))
    return jnp.stack(results)

def contract(left, right):
    return lax.dot_general(left, right, (((1,), (1,)), ((), ())), preferred_element_type=jnp.float32)

def squared(hidden):
    wide_value = hidden.astype(jnp.float32)
    return wide_value * wide_value

def collide_forward(state, w_in, w_mid, w_out):
    inputs_bf = state.astype(jnp.bfloat16)
    layers = [jnp.tanh(jnp.dot(w_in, inputs_bf, preferred_element_type=jnp.float32)).astype(jnp.bfloat16)]
    for depth in range(w_mid.shape[0]):
        layers.append(jnp.tanh(jnp.dot(w_mid[depth], layers[-1], preferred_element_type=jnp.float32)).astype(jnp.bfloat16))
    collided = state + jnp.dot(w_out, layers[-1], preferred_element_type=jnp.float32)
    return (collided, inputs_bf, layers)

def collide_backward(collided_bar, inputs_bf, layers, w_in, w_mid, w_out):
    delta_bf = collided_bar.astype(jnp.bfloat16)
    grad_out = contract(delta_bf, layers[-1])
    signal = (jnp.dot(w_out.T, delta_bf, preferred_element_type=jnp.float32) * (1.0 - squared(layers[-1]))).astype(jnp.bfloat16)
    mid_parts = []
    for depth in reversed(range(w_mid.shape[0])):
        mid_parts.insert(0, contract(signal, layers[depth]))
        signal = (jnp.dot(w_mid[depth].T, signal, preferred_element_type=jnp.float32) * (1.0 - squared(layers[depth]))).astype(jnp.bfloat16)
    grad_in = contract(signal, inputs_bf)
    state_bar = collided_bar + jnp.dot(w_in.T, signal, preferred_element_type=jnp.float32)
    return (state_bar, grad_in, jnp.stack(mid_parts), grad_out)

def stream_all(collided, face_source, face_level, face_quadrant):
    outward = jax.vmap(jax.vmap(partial(face_layers, block_side=S)))(collided)
    lateral = [jnp.take(outward[:, :, face_id ^ 1], face_source[:, face_id], axis=1) for face_id in range(4)]
    from_above = jnp.roll(outward[:, :, 5], -1, axis=0)
    from_below = jnp.roll(outward[:, :, 4], 1, axis=0)
    sheets = jnp.stack(lateral + [from_above, from_below], axis=2)
    ghosts = jax.vmap(jax.vmap(jax.vmap(partial(refine_sheet, block_side=S))))(sheets, face_level, face_quadrant)
    return jax.vmap(jax.vmap(partial(stream_block, block_side=S)))(collided, ghosts)

def reference(populations, w_in, w_mid, w_out, cotangent, face_source, face_level, face_quadrant):
    state = jnp.transpose(populations, (1, 2, 0, 3))
    whole_shape = state.shape
    flat_shape = (whole_shape[0] * whole_shape[1], Q, CELLS)
    streamer = partial(stream_all, face_source=face_source, face_level=face_level, face_quadrant=face_quadrant)

    def collide_one(block):
        return collide_forward(block, w_in, w_mid, w_out)[0]

    def pull_one(pair):
        block, upstream = pair
        collided, inputs_bf, layers = collide_forward(block, w_in, w_mid, w_out)
        return collide_backward(upstream, inputs_bf, layers, w_in, w_mid, w_out)
    history = []
    for step_id in range(STEPS):
        history.append(state)
        collided = lax.map(collide_one, state.reshape(flat_shape)).reshape(whole_shape)
        state = streamer(collided)
    final_state = state
    state_bar = jnp.transpose(cotangent, (1, 2, 0, 3))
    total_in = jnp.zeros((HID, Q), jnp.float32)
    total_mid = jnp.zeros((MIDS, HID, HID), jnp.float32)
    total_out = jnp.zeros((Q, HID), jnp.float32)
    for step_id in reversed(range(STEPS)):
        earlier_state = history[step_id]
        collided = lax.map(collide_one, earlier_state.reshape(flat_shape)).reshape(whole_shape)
        unused, stream_pull = jax.vjp(streamer, collided)
        collided_bar, = stream_pull(state_bar)
        flat_bar, part_in, part_mid, part_out = lax.map(pull_one, (earlier_state.reshape(flat_shape), collided_bar.reshape(flat_shape)))
        state_bar = flat_bar.reshape(whole_shape)
        total_in = total_in + lax.optimization_barrier(jnp.sum(part_in, axis=0))
        total_mid = total_mid + lax.optimization_barrier(jnp.sum(part_mid, axis=0))
        total_out = total_out + lax.optimization_barrier(jnp.sum(part_out, axis=0))
    grad_scale = float(CELLS_ALL) ** (-0.5)
    return (jnp.transpose(final_state, (2, 0, 1, 3)), jnp.transpose(state_bar, (2, 0, 1, 3)), total_in * grad_scale, total_mid * grad_scale, total_out * grad_scale)
```

```python
import functools

import jax
import jax.numpy as jnp
import numpy as np
from jax import lax
from jax.experimental import pallas as pl
from jax.experimental.pallas import tpu as pltpu
from jax.sharding import PartitionSpec as P

REACH = 3
R = 24
S = 16
A = S * S
CHUNK = 512
MESH = pl.DeviceIdType.MESH
F32, BF16 = jnp.float32, jnp.bfloat16

VELOCITIES = [
    (0, 0, 0),
    (1, 0, 0),
    (-1, 0, 0),
    (0, 1, 0),
    (0, -1, 0),
    (0, 0, 1),
    (0, 0, -1),
    (1, 1, 0),
    (-1, -1, 0),
    (1, -1, 0),
    (-1, 1, 0),
    (1, 0, 1),
    (-1, 0, -1),
    (1, 0, -1),
    (-1, 0, 1),
    (0, 1, 1),
    (0, -1, -1),
    (0, 1, -1),
    (0, -1, 1),
]
Q = len(VELOCITIES)


def row_table():
    table = np.zeros((4, R, A), np.int32)
    for q, v in enumerate(VELOCITIES):
        for axis in range(3):
            table[axis, q] = v[axis]
        if q:
            table[3, q] = 1 if q % 2 else -1
    return table


def lane_roll(x, shift):
    shift %= A
    return x if shift == 0 else pltpu.roll(x, shift, 1)


class Geometry:
    def __init__(self, table_ref):
        lane = lax.broadcasted_iota(jnp.int32, (R, A), 1)
        y, z = lane // S, lane % S
        self.v = [table_ref[axis] for axis in range(3)]
        self.plus = [v == 1 for v in self.v]
        self.minus = [v == -1 for v in self.v]
        parity = table_ref[3]
        self.odd, self.even = parity == 1, parity == -1
        py, my, pz, mz = self.plus[1], self.minus[1], self.plus[2], self.minus[2]
        self.ly = (py & (y == 0)) | (my & (y == S - 1))
        self.lz = (pz & (z == 0)) | (mz & (z == S - 1))
        self.oy = (py & (y == S - 1)) | (my & (y == 0))
        self.oz = (pz & (z == S - 1)) | (mz & (z == 0))

    def row_roll(self, x, axis, step, sign=1):
        up, down = lane_roll(x, sign * step), lane_roll(x, -sign * step)
        return jnp.where(self.plus[axis], up, jnp.where(self.minus[axis], down, x))

    def opposite(self, x):
        return jnp.where(self.odd, pltpu.roll(x, R - 1, 0), jnp.where(self.even, pltpu.roll(x, 1, 0), x))

    def leaving_x(self, k):
        if k == 0:
            return self.plus[0]
        if k == S - 1:
            return self.minus[0]
        return None

    def crossings(self, k):
        ly, lz, lx = self.ly, self.lz, self.leaving_x(k)
        two, some = ly & lz, ly | lz
        if lx is None:
            return ly & ~lz, lz & ~ly, None, two, ~some
        return (
            ly & ~lz & ~lx,
            lz & ~ly & ~lx,
            lx & ~some,
            two | (lx & some),
            ~(some | lx),
        )


def layer(ref, k):
    return ref[:, k * A : (k + 1) * A]


def put(ref, k, value):
    ref[:, k * A : (k + 1) * A] = value


def split3(x):
    hi = x.astype(BF16)
    rest = x - hi.astype(F32)
    mid = rest.astype(BF16)
    low = (rest - mid.astype(F32)).astype(BF16)
    return jnp.concatenate([hi, mid, low], axis=0)


def refine(g, sheet, axis, pick_ref, transposed):
    parts = split3(sheet)
    dims = (((1,), (1 if transposed else 0,)), ((), ()))
    both = []
    for face in (2 * axis, 2 * axis + 1):
        r = lax.dot_general(parts, pick_ref[face], dims, preferred_element_type=F32)
        both.append(r[:R] + r[R : 2 * R] + r[2 * R :])
    return jnp.where(g.minus[axis], both[0], both[1])


def gather_sheets(g, ref, sheets_ref):
    acc_y = acc_z = None
    for k in range(S):
        a = layer(ref, k)
        ty = lane_roll(jnp.where(g.oy, a, 0.0), S * k)
        tz = lane_roll(jnp.where(g.oz, a, 0.0), k)
        acc_y = ty if acc_y is None else acc_y + ty
        acc_z = tz if acc_z is None else acc_z + tz
    sheet_x = jnp.where(g.plus[0], layer(ref, S - 1), jnp.where(g.minus[0], layer(ref, 0), 0.0))
    sheets_ref[0, :R] = sheet_x
    sheets_ref[1, :R] = jnp.where(g.plus[1], lane_roll(acc_y, S), acc_y)
    sheets_ref[2, :R] = jnp.where(g.plus[2], lane_roll(acc_z, -(S - 1)), acc_z)


def gather_bars(g, ref, pick_ref, sheets_ref):
    acc_x = acc_y = acc_z = None
    for k in range(S):
        b = layer(ref, k)
        one_y, one_z, one_x, _, _ = g.crossings(k)
        ty = lane_roll(jnp.where(one_y, b, 0.0), S * k)
        tz = lane_roll(jnp.where(one_z, b, 0.0), k)
        acc_y = ty if acc_y is None else acc_y + ty
        acc_z = tz if acc_z is None else acc_z + tz
        if one_x is not None:
            tx = jnp.where(one_x, b, 0.0)
            acc_x = tx if acc_x is None else acc_x + tx
    acc_y = jnp.where(g.minus[1], lane_roll(acc_y, S), acc_y)
    acc_z = jnp.where(g.minus[2], lane_roll(acc_z, -(S - 1)), acc_z)
    gx = g.row_roll(g.row_roll(acc_x, 1, S, -1), 2, 1, -1)
    gy = g.row_roll(g.row_roll(acc_y, 0, S, -1), 2, 1, -1)
    gz = g.row_roll(g.row_roll(acc_z, 1, S, -1), 0, 1, -1)
    for axis, value in enumerate((gx, gy, gz)):
        sheets_ref[axis, R:] = refine(g, value, axis, pick_ref, True)


def stream(g, post_ref, recv_ref, slot_ref, pick_ref, out_ref, rows):
    from_plus, from_minus = recv_ref[slot_ref[0], :R], recv_ref[slot_ref[1], :R]
    raw_x = jnp.where(g.minus[0], from_plus, from_minus)
    raw_y = recv_ref[2 * REACH, :R]
    raw_z = jnp.where(g.minus[2], recv_ref[2 * REACH + 1, :R], recv_ref[2 * REACH + 2, :R])
    gx, gy, gz = (refine(g, raw, axis, pick_ref, False) for axis, raw in enumerate((raw_x, raw_y, raw_z)))
    sx = g.row_roll(g.row_roll(gx, 1, S), 2, 1)
    sy = g.row_roll(g.row_roll(gy, 0, S), 2, 1)
    sz = g.row_roll(g.row_roll(gz, 1, S), 0, 1)
    sy = jnp.where(g.minus[1], lane_roll(sy, -S), sy)
    sz = jnp.where(g.minus[2], lane_roll(sz, S - 1), sz)
    for k in range(S):
        here = layer(post_ref, k)
        behind = layer(post_ref, max(k - 1, 0))
        ahead = layer(post_ref, min(k + 1, S - 1))
        moved = jnp.where(g.plus[0], behind, jnp.where(g.minus[0], ahead, here))
        moved = g.row_roll(g.row_roll(moved, 1, S), 2, 1)
        one_y, one_z, one_x, two, _ = g.crossings(k)
        out = jnp.where(one_y, lane_roll(sy, -S * k), moved)
        out = jnp.where(one_z, lane_roll(sz, -k), out)
        if one_x is not None:
            out = jnp.where(one_x, sx, out)
        out = jnp.where(two, g.opposite(here), out)
        out_ref[:, k * A : (k + 1) * A] = out[:rows]


def stream_back(g, bar_ref, recv_ref, slot_ref, work_ref, out_ref):
    from_plus, from_minus = recv_ref[slot_ref[0], R:], recv_ref[slot_ref[1], R:]
    ox = jnp.where(g.plus[0], from_plus, from_minus)
    oy = recv_ref[2 * REACH, R:]
    oz = jnp.where(g.plus[2], recv_ref[2 * REACH + 1, R:], recv_ref[2 * REACH + 2, R:])
    oy = jnp.where(g.plus[1], lane_roll(oy, -S), oy)
    oz = jnp.where(g.plus[2], lane_roll(oz, S - 1), oz)
    for k in range(S):
        put(work_ref, k, jnp.where(g.crossings(k)[4], layer(bar_ref, k), 0.0))
    for k in range(S):
        zero = jnp.zeros((R, A), F32)
        ahead = layer(work_ref, k + 1) if k + 1 < S else zero
        behind = layer(work_ref, k - 1) if k > 0 else zero
        moved = jnp.where(g.plus[0], ahead, jnp.where(g.minus[0], behind, layer(work_ref, k)))
        out = g.row_roll(g.row_roll(moved, 1, S, -1), 2, 1, -1)
        out += g.opposite(jnp.where(g.crossings(k)[3], layer(bar_ref, k), 0.0))
        out += jnp.where(g.oy, lane_roll(oy, -S * k), 0.0)
        out += jnp.where(g.oz, lane_roll(oz, -k), 0.0)
        if k == 0:
            out += jnp.where(g.minus[0], ox, 0.0)
        if k == S - 1:
            out += jnp.where(g.plus[0], ox, 0.0)
        put(out_ref, k, out)


def mm(a, b):
    return jnp.dot(a, b, preferred_element_type=F32)


def outer(a, b):
    return lax.dot_general(a, b, (((1,), (1,)), ((), ())), preferred_element_type=F32)


def slope(h):
    wide = h.astype(F32)
    return 1.0 - wide * wide


def collide(x, w_in, w_mid, w_out):
    inputs = x.astype(BF16)
    h0 = jnp.tanh(mm(w_in[...], inputs)).astype(BF16)
    h1 = jnp.tanh(mm(w_mid[...], h0)).astype(BF16)
    return inputs, h0, h1, x + mm(w_out[...], h1)


def collide_back(bar, inputs, h0, h1, w_in_t, w_mid_t, w_out_t, grads_ref, hid):
    e = bar.astype(BF16)
    a1 = (mm(w_out_t[...], e) * slope(h1)).astype(BF16)
    a0 = (mm(w_mid_t[...], a1) * slope(h0)).astype(BF16)
    grads_ref[:hid] += outer(a1, h0)
    grads_ref[hid : hid + R] += outer(inputs, a0)
    grads_ref[hid + R : hid + 2 * R] += outer(e, h1)
    return bar + mm(w_in_t[...], a0)


def span(i):
    return pl.ds(pl.multiple_of(i * CHUNK, CHUNK), CHUNK)


def load_rows(dst, src):
    dst[...] = jnp.zeros(dst.shape, F32)
    dst[:Q] = src[...]


def first_kernel(
    table, pick, pops, cot, w_in, w_mid, w_out, post, h_hbm, sheets, wide, cot_wide, h_buf, sems
):
    g = Geometry(table)
    cells = pops.shape[1]
    load_rows(wide, pops)
    load_rows(cot_wide, cot)

    def moved(i, j):
        return pltpu.make_async_copy(h_buf.at[j, :, span(i)], h_hbm.at[j, :, span(i)], sems.at[j, i])

    @pl.loop(0, cells // CHUNK)
    def _(i):
        at = span(i)
        _, h0, h1, out = collide(wide[:, at], w_in, w_mid, w_out)
        post[:, at] = out
        h_buf[0, :, at] = h0
        h_buf[1, :, at] = h1
        moved(i, 0).start()
        moved(i, 1).start()

    gather_sheets(g, post, sheets)
    gather_bars(g, cot_wide, pick, sheets)

    @pl.loop(0, cells // CHUNK)
    def _(i):
        moved(i, 0).wait()
        moved(i, 1).wait()


def middle_kernel(
    slots, table, pick, recv, post1, cot, w_in, w_mid, w_out, w_in_t, w_mid_t, w_out_t,
    post2, bar, sheets, grads, state, wide, work, pbar,
):
    g = Geometry(table)
    cells = post1.shape[1]
    hid = w_mid.shape[0]
    load_rows(wide, cot)
    stream(g, post1, recv, slots, pick, state, R)
    stream_back(g, wide, recv, slots, work, pbar)
    grads[...] = jnp.zeros(grads.shape, F32)

    @pl.loop(0, cells // CHUNK)
    def _(i):
        at = span(i)
        inputs, h0, h1, out = collide(state[:, at], w_in, w_mid, w_out)
        post2[:, at] = out
        bar[:, at] = collide_back(pbar[:, at], inputs, h0, h1, w_in_t, w_mid_t, w_out_t, grads, hid)

    gather_sheets(g, post2, sheets)
    gather_bars(g, bar, pick, sheets)


def last_kernel(
    slots, table, pick, recv, post2, bar, pops, h_hbm, grads_in, w_in_t, w_mid_t, w_out_t,
    final, grad_pops, grads, wide, work, pbar, h_buf, sems,
):
    g = Geometry(table)
    cells = post2.shape[1]
    hid = w_mid_t.shape[0]

    def moved(i, j):
        return pltpu.make_async_copy(h_hbm.at[j, :, span(i)], h_buf.at[j, :, span(i)], sems.at[j, i])

    @pl.loop(0, cells // CHUNK)
    def _(i):
        moved(i, 0).start()
        moved(i, 1).start()

    load_rows(wide, pops)
    stream(g, post2, recv, slots, pick, final, Q)
    stream_back(g, bar, recv, slots, work, pbar)
    grads[...] = grads_in[...]

    @pl.loop(0, cells // CHUNK)
    def _(i):
        at = span(i)
        moved(i, 0).wait()
        moved(i, 1).wait()
        out = collide_back(
            pbar[:, at], wide[:, at].astype(BF16), h_buf[0, :, at], h_buf[1, :, at],
            w_in_t, w_mid_t, w_out_t, grads, hid,
        )
        grad_pops[:, at] = out[:Q]


OFFSETS = [d for d in range(-REACH, REACH + 1) if d != 0]


def exchange_kernel(blocks, slabs, sheets, recv, send_sem, recv_sem):
    me, level = lax.axis_index("blocks"), lax.axis_index("slab")
    side = [lax.rem(me - d + blocks, blocks) for d in OFFSETS]
    other = me + 1 - 2 * lax.rem(me, 2)
    above, below = lax.rem(level + 1, slabs), lax.rem(level + slabs - 1, slabs)
    barrier = pltpu.get_barrier_semaphore()
    for target in side:
        pl.semaphore_signal(barrier, inc=1, device_id={"blocks": target}, device_id_type=MESH)
    for target in (above, below):
        pl.semaphore_signal(barrier, inc=1, device_id={"slab": target}, device_id_type=MESH)
    pl.semaphore_wait(barrier, len(side) + 2)
    plan = [(0, i, {"blocks": target}) for i, target in enumerate(side)]
    plan.append((1, len(side), {"blocks": other}))
    plan.append((2, len(side) + 1, {"slab": below}))
    plan.append((2, len(side) + 2, {"slab": above}))
    copies = []
    for which, slot, device in plan:
        copy = pltpu.make_async_remote_copy(
            src_ref=sheets.at[which], dst_ref=recv.at[slot],
            send_sem=send_sem.at[slot], recv_sem=recv_sem.at[slot],
            device_id=device, device_id_type=MESH,
        )
        copy.start()
        copies.append(copy)
    for copy in copies:
        copy.wait()


def sum_kernel(blocks, slabs, grads, out, land_b, land_s, part, sems_b, sems_s, gath_b, gath_s):
    me, level = lax.axis_index("blocks"), lax.axis_index("slab")
    rows, width = grads.shape[0] // blocks, grads.shape[1] // slabs
    barrier = pltpu.get_barrier_semaphore()
    peer_b = [lax.rem(me + d, blocks) for d in range(1, blocks)]
    peer_s = [lax.rem(level + d, slabs) for d in range(1, slabs)]
    for t in peer_b:
        pl.semaphore_signal(barrier, inc=1, device_id={"blocks": t}, device_id_type=MESH)
    for t in peer_s:
        pl.semaphore_signal(barrier, inc=1, device_id={"slab": t}, device_id_type=MESH)
    pl.semaphore_wait(barrier, blocks + slabs - 2)

    def row_of(i):
        return pl.ds(pl.multiple_of(i * rows, 8), rows)

    def lane_of(i):
        return pl.ds(pl.multiple_of(i * width, 128), width)

    def send(src, dst, sems, i, axis, target):
        copy = pltpu.make_async_remote_copy(
            src_ref=src, dst_ref=dst, send_sem=sems.at[0, i], recv_sem=sems.at[1, i],
            device_id={axis: target}, device_id_type=MESH,
        )
        copy.start()
        return copy

    copies = [send(grads.at[row_of(t)], land_b.at[i], sems_b, i, "blocks", t) for i, t in enumerate(peer_b)]
    total = grads[row_of(me)]
    for i, copy in enumerate(copies):
        copy.wait()
        total += land_b[i]
    part[...] = total
    copies = [send(part.at[:, lane_of(t)], land_s.at[i], sems_s, i, "slab", t) for i, t in enumerate(peer_s)]
    mine = part[:, lane_of(level)]
    for i, copy in enumerate(copies):
        copy.wait()
        mine += land_s[i]
    out[row_of(me), lane_of(level)] = mine
    spot = out.at[row_of(me), lane_of(level)]
    copies = [send(spot, spot, gath_s, i, "slab", t) for i, t in enumerate(peer_s)]
    for copy in copies:
        copy.wait()
    spot = out.at[row_of(me)]
    copies = [send(spot, spot, gath_b, i, "blocks", t) for i, t in enumerate(peer_b)]
    for copy in copies:
        copy.wait()


def pickers(levels, quadrant):
    swapped = quadrant % 2 * 2 + quadrant // 2
    quadrant = jnp.where(jnp.arange(6) >= 4, swapped, quadrant)
    target = lax.iota(jnp.int32, A)
    row, col = target // S, target % S
    half = S // 2
    src = (quadrant[:, None] // 2 * half + row // 2) * S + quadrant[:, None] % 2 * half + col // 2
    source = jnp.where(levels[:, None] == 1, src, target[None, :])
    return (target[None, :, None] == source[:, None, :]).astype(BF16)


def vmem(count):
    return [pl.BlockSpec(memory_space=pltpu.VMEM)] * count


SMEM_SPEC = pl.BlockSpec(memory_space=pltpu.SMEM)
ANY_SPEC = pl.BlockSpec(memory_space=pl.ANY)
LIMIT = 60 * 1024 * 1024


def shape(dims, dtype=F32):
    return jax.ShapeDtypeStruct(dims, dtype)


def shards(blocks, slabs, populations, w_in, w_mid, w_out, cotangent, face_source, face_level, face_quadrant):
    cells = populations.shape[-1]
    hid = w_in.shape[0]
    pops, cot = populations[:, 0, 0, :], cotangent[:, 0, 0, :]
    table = jnp.asarray(row_table())
    pick = pickers(face_level[0, 0], face_quadrant[0, 0])
    position = lax.axis_index("blocks")
    neighbours = lax.dynamic_index_in_dim(face_source, position, 0, keepdims=False)
    distance = (neighbours - position + blocks) % blocks
    distance = jnp.where(distance > blocks // 2, distance - blocks, distance)
    slots = jnp.where(distance < 0, distance + REACH, distance + REACH - 1)[:2]
    slots = jnp.clip(slots, 0, 2 * REACH - 1)
    w_in = jnp.pad(w_in, ((0, 0), (0, R - Q)))
    w_out = jnp.pad(w_out, ((0, R - Q), (0, 0)))
    w_mid = w_mid[0]
    backs = (w_in.T, w_mid.T, w_out.T)
    step = 8 * blocks
    total_rows = -(-(hid + 2 * R) // step) * step
    parts = cells // CHUNK
    volume = pltpu.VMEM((R, cells), F32)
    params = pltpu.CompilerParams(vmem_limit_bytes=LIMIT)

    def exchange(sheets, which):
        count = 2 * REACH + 3
        return pl.pallas_call(
            functools.partial(exchange_kernel, blocks, slabs),
            out_shape=shape((count, 2 * R, A)),
            in_specs=vmem(1),
            out_specs=vmem(1)[0],
            scratch_shapes=[pltpu.SemaphoreType.DMA((count,)), pltpu.SemaphoreType.DMA((count,))],
            compiler_params=pltpu.CompilerParams(collective_id=which, has_side_effects=True),
            name=f"exchange{which}",
        )(sheets)

    post1, hidden, sheets = pl.pallas_call(
        first_kernel,
        out_shape=(shape((R, cells)), shape((2, hid, cells), BF16), shape((3, 2 * R, A))),
        in_specs=vmem(7),
        out_specs=(vmem(1)[0], ANY_SPEC, vmem(1)[0]),
        scratch_shapes=[volume, volume, pltpu.VMEM((2, hid, cells), BF16), pltpu.SemaphoreType.DMA((2, parts))],
        compiler_params=params,
        name="first",
    )(table, pick, pops, cot, w_in, w_mid, w_out)
    recv = exchange(sheets, 0)
    post2, bar, sheets, grads = pl.pallas_call(
        middle_kernel,
        out_shape=(shape((R, cells)), shape((R, cells)), shape((3, 2 * R, A)), shape((total_rows, hid))),
        in_specs=[SMEM_SPEC] + vmem(11),
        out_specs=tuple(vmem(4)),
        scratch_shapes=[volume] * 4,
        compiler_params=params,
        name="middle",
    )(slots, table, pick, recv, post1, cot, w_in, w_mid, w_out, *backs)
    recv = exchange(sheets, 1)
    final, grad_pops, grads = pl.pallas_call(
        last_kernel,
        out_shape=(shape((Q, cells)), shape((Q, cells)), shape((total_rows, hid))),
        in_specs=[SMEM_SPEC] + vmem(6) + [ANY_SPEC] + vmem(4),
        out_specs=tuple(vmem(3)),
        scratch_shapes=[volume] * 3 + [pltpu.VMEM((2, hid, cells), BF16), pltpu.SemaphoreType.DMA((2, parts))],
        compiler_params=params,
        name="last",
    )(slots, table, pick, recv, post2, bar, pops, hidden, grads, *backs)
    rows, width = total_rows // blocks, hid // slabs
    total = pl.pallas_call(
        functools.partial(sum_kernel, blocks, slabs),
        out_shape=shape((total_rows, hid)),
        in_specs=vmem(1),
        out_specs=vmem(1)[0],
        scratch_shapes=[
            pltpu.VMEM((blocks - 1, rows, hid), F32),
            pltpu.VMEM((slabs - 1, rows, width), F32),
            pltpu.VMEM((rows, hid), F32),
            pltpu.SemaphoreType.DMA((2, blocks - 1)),
            pltpu.SemaphoreType.DMA((2, slabs - 1)),
            pltpu.SemaphoreType.DMA((2, blocks - 1)),
            pltpu.SemaphoreType.DMA((2, slabs - 1)),
        ],
        compiler_params=pltpu.CompilerParams(collective_id=2, has_side_effects=True),
        name="sum_all",
    )(grads)
    total = total * float(blocks * slabs * cells) ** (-0.5)
    return (
        final[:, None, None, :],
        grad_pops[:, None, None, :],
        total[hid : hid + Q].T,
        total[:hid][None],
        total[hid + R : hid + R + Q],
    )


def solution(mesh):
    spread = P(None, "slab", "blocks", None)
    in_specs = (spread, P(), P(), P(), spread, P(), P("slab", "blocks", None), P("slab", "blocks", None))
    out_specs = (spread, spread, P(), P(), P())
    body = functools.partial(shards, mesh.shape["blocks"], mesh.shape["slab"])
    return jax.shard_map(body, mesh=mesh, in_specs=in_specs, out_specs=out_specs, check_vma=False)
```

```python
import functools

import jax
import jax.numpy as jnp
import numpy as np
from jax import lax
from jax.experimental import pallas as pl
from jax.experimental.pallas import tpu as pltpu
from jax.sharding import PartitionSpec as P

REACH = 3
R = 24
S = 16
A = S * S
CHUNK = 512
MESH = pl.DeviceIdType.MESH
F32, BF16 = jnp.float32, jnp.bfloat16

VELOCITIES = [
    (0, 0, 0),
    (1, 0, 0),
    (-1, 0, 0),
    (0, 1, 0),
    (0, -1, 0),
    (0, 0, 1),
    (0, 0, -1),
    (1, 1, 0),
    (-1, -1, 0),
    (1, -1, 0),
    (-1, 1, 0),
    (1, 0, 1),
    (-1, 0, -1),
    (1, 0, -1),
    (-1, 0, 1),
    (0, 1, 1),
    (0, -1, -1),
    (0, 1, -1),
    (0, -1, 1),
]
Q = len(VELOCITIES)


def row_table():
    table = np.zeros((4, R, A), np.int32)
    for q, v in enumerate(VELOCITIES):
        for axis in range(3):
            table[axis, q] = v[axis]
        if q:
            table[3, q] = 1 if q % 2 else -1
    return table


def lane_roll(x, shift):
    shift %= A
    return x if shift == 0 else pltpu.roll(x, shift, 1)


class Geometry:
    def __init__(self, table_ref):
        lane = lax.broadcasted_iota(jnp.int32, (R, A), 1)
        y, z = lane // S, lane % S
        self.v = [table_ref[axis] for axis in range(3)]
        self.plus = [v == 1 for v in self.v]
        self.minus = [v == -1 for v in self.v]
        parity = table_ref[3]
        self.odd, self.even = parity == 1, parity == -1
        py, my, pz, mz = self.plus[1], self.minus[1], self.plus[2], self.minus[2]
        self.ly = (py & (y == 0)) | (my & (y == S - 1))
        self.lz = (pz & (z == 0)) | (mz & (z == S - 1))
        self.oy = (py & (y == S - 1)) | (my & (y == 0))
        self.oz = (pz & (z == S - 1)) | (mz & (z == 0))

    def row_roll(self, x, axis, step, sign=1):
        up, down = lane_roll(x, sign * step), lane_roll(x, -sign * step)
        return jnp.where(self.plus[axis], up, jnp.where(self.minus[axis], down, x))

    def opposite(self, x):
        return jnp.where(self.odd, pltpu.roll(x, R - 1, 0), jnp.where(self.even, pltpu.roll(x, 1, 0), x))

    def leaving_x(self, k):
        if k == 0:
            return self.plus[0]
        if k == S - 1:
            return self.minus[0]
        return None

    def crossings(self, k):
        ly, lz, lx = self.ly, self.lz, self.leaving_x(k)
        two, some = ly & lz, ly | lz
        if lx is None:
            return ly & ~lz, lz & ~ly, None, two, ~some
        return (
            ly & ~lz & ~lx,
            lz & ~ly & ~lx,
            lx & ~some,
            two | (lx & some),
            ~(some | lx),
        )


def layer(ref, k):
    return ref[:, k * A : (k + 1) * A]


def put(ref, k, value):
    ref[:, k * A : (k + 1) * A] = value


def split3(x):
    hi = x.astype(BF16)
    rest = x - hi.astype(F32)
    mid = rest.astype(BF16)
    low = (rest - mid.astype(F32)).astype(BF16)
    return jnp.concatenate([hi, mid, low], axis=0)


def refine(g, sheet, axis, pick_ref, transposed):
    parts = split3(sheet)
    dims = (((1,), (1 if transposed else 0,)), ((), ()))
    both = []
    for face in (2 * axis, 2 * axis + 1):
        r = lax.dot_general(parts, pick_ref[face], dims, preferred_element_type=F32)
        both.append(r[:R] + r[R : 2 * R] + r[2 * R :])
    return jnp.where(g.minus[axis], both[0], both[1])


PACK = [
    [(0, 1, 3), (2, 7, 15)],
    [(0, 3, 5), (2, 7, 11), (6, 15, 19)],
    [(0, 5, 7), (2, 11, 19)],
]
FACED = 10


def pack(sheets_ref, axis, base, value):
    for at, low, high in PACK[axis]:
        sheets_ref[axis, base + at : base + at + high - low] = value[low:high]


def unpack(recv_ref, slot, axis, base, tmp_ref):
    tmp_ref[...] = jnp.zeros(tmp_ref.shape, F32)
    for at, low, high in PACK[axis]:
        tmp_ref[low:high] = recv_ref[slot, base + at : base + at + high - low]
    return tmp_ref[...]


def slot_of(source_ref, blocks, face):
    me = lax.axis_index("blocks")
    distance = lax.rem(source_ref[me, face] - me + blocks, blocks)
    distance = jnp.where(distance > blocks // 2, distance - blocks, distance)
    slot = jnp.where(distance < 0, distance + REACH, distance + REACH - 1)
    return jnp.clip(slot, 0, 2 * REACH - 1)


def gather_sheets(g, ref, sheets_ref):
    acc_y = acc_z = None
    for k in range(S):
        a = layer(ref, k)
        ty = lane_roll(jnp.where(g.oy, a, 0.0), S * k)
        tz = lane_roll(jnp.where(g.oz, a, 0.0), k)
        acc_y = ty if acc_y is None else acc_y + ty
        acc_z = tz if acc_z is None else acc_z + tz
    sheet_x = jnp.where(g.plus[0], layer(ref, S - 1), jnp.where(g.minus[0], layer(ref, 0), 0.0))
    pack(sheets_ref, 0, 0, sheet_x)
    pack(sheets_ref, 1, 0, jnp.where(g.plus[1], lane_roll(acc_y, S), acc_y))
    pack(sheets_ref, 2, 0, jnp.where(g.plus[2], lane_roll(acc_z, -(S - 1)), acc_z))


def gather_bars(g, ref, pick_ref, sheets_ref):
    acc_x = acc_y = acc_z = None
    for k in range(S):
        b = layer(ref, k)
        one_y, one_z, one_x, _, _ = g.crossings(k)
        ty = lane_roll(jnp.where(one_y, b, 0.0), S * k)
        tz = lane_roll(jnp.where(one_z, b, 0.0), k)
        acc_y = ty if acc_y is None else acc_y + ty
        acc_z = tz if acc_z is None else acc_z + tz
        if one_x is not None:
            tx = jnp.where(one_x, b, 0.0)
            acc_x = tx if acc_x is None else acc_x + tx
    acc_y = jnp.where(g.minus[1], lane_roll(acc_y, S), acc_y)
    acc_z = jnp.where(g.minus[2], lane_roll(acc_z, -(S - 1)), acc_z)
    gx = g.row_roll(g.row_roll(acc_x, 1, S, -1), 2, 1, -1)
    gy = g.row_roll(g.row_roll(acc_y, 0, S, -1), 2, 1, -1)
    gz = g.row_roll(g.row_roll(acc_z, 1, S, -1), 0, 1, -1)
    for axis, value in enumerate((gx, gy, gz)):
        pack(sheets_ref, axis, FACED, refine(g, value, axis, pick_ref, True))


def received(g, recv_ref, slots, base, toward, tmp_ref):
    sides = [unpack(recv_ref, slot, 0, base, tmp_ref) for slot in slots]
    x = jnp.where(toward[0], sides[0], sides[1])
    y = unpack(recv_ref, 2 * REACH, 1, base, tmp_ref)
    sides = [unpack(recv_ref, 2 * REACH + side, 2, base, tmp_ref) for side in (1, 2)]
    return x, y, jnp.where(toward[2], sides[0], sides[1])


def stream(g, post_ref, recv_ref, slots, pick_ref, tmp_ref, store):
    raw_x, raw_y, raw_z = received(g, recv_ref, slots, 0, g.minus, tmp_ref)
    gx, gy, gz = (refine(g, raw, axis, pick_ref, False) for axis, raw in enumerate((raw_x, raw_y, raw_z)))
    sx = g.row_roll(g.row_roll(gx, 1, S), 2, 1)
    sy = g.row_roll(g.row_roll(gy, 0, S), 2, 1)
    sz = g.row_roll(g.row_roll(gz, 1, S), 0, 1)
    sy = jnp.where(g.minus[1], lane_roll(sy, -S), sy)
    sz = jnp.where(g.minus[2], lane_roll(sz, S - 1), sz)
    for k in range(S):
        here = layer(post_ref, k)
        behind = layer(post_ref, max(k - 1, 0))
        ahead = layer(post_ref, min(k + 1, S - 1))
        moved = jnp.where(g.plus[0], behind, jnp.where(g.minus[0], ahead, here))
        moved = g.row_roll(g.row_roll(moved, 1, S), 2, 1)
        one_y, one_z, one_x, two, _ = g.crossings(k)
        out = jnp.where(one_y, lane_roll(sy, -S * k), moved)
        out = jnp.where(one_z, lane_roll(sz, -k), out)
        if one_x is not None:
            out = jnp.where(one_x, sx, out)
        out = jnp.where(two, g.opposite(here), out)
        store(k, out)


def stream_back(g, bar_ref, recv_ref, slots, tmp_ref, work_ref, out_ref):
    ox, oy, oz = received(g, recv_ref, slots, FACED, g.plus, tmp_ref)
    oy = jnp.where(g.plus[1], lane_roll(oy, -S), oy)
    oz = jnp.where(g.plus[2], lane_roll(oz, S - 1), oz)
    for k in range(S):
        put(work_ref, k, jnp.where(g.crossings(k)[4], layer(bar_ref, k), 0.0))
    for k in range(S):
        zero = jnp.zeros((R, A), F32)
        ahead = layer(work_ref, k + 1) if k + 1 < S else zero
        behind = layer(work_ref, k - 1) if k > 0 else zero
        moved = jnp.where(g.plus[0], ahead, jnp.where(g.minus[0], behind, layer(work_ref, k)))
        out = g.row_roll(g.row_roll(moved, 1, S, -1), 2, 1, -1)
        out += g.opposite(jnp.where(g.crossings(k)[3], layer(bar_ref, k), 0.0))
        out += jnp.where(g.oy, lane_roll(oy, -S * k), 0.0)
        out += jnp.where(g.oz, lane_roll(oz, -k), 0.0)
        if k == 0:
            out += jnp.where(g.minus[0], ox, 0.0)
        if k == S - 1:
            out += jnp.where(g.plus[0], ox, 0.0)
        put(out_ref, k, out)


def mm(a, b):
    return jnp.dot(a, b, preferred_element_type=F32)


def outer(a, b):
    return lax.dot_general(a, b, (((1,), (1,)), ((), ())), preferred_element_type=F32)


def slope(h):
    wide = h.astype(F32)
    return 1.0 - wide * wide


def collide(x, w_in, w_mid, w_out):
    inputs = x.astype(BF16)
    h0 = jnp.tanh(mm(w_in[...], inputs)).astype(BF16)
    h1 = jnp.tanh(mm(w_mid[...], h0)).astype(BF16)
    return inputs, h0, h1, x + mm(w_out[...], h1)


def collide_back(bar, inputs, h0, h1, w_in_t, w_mid_t, w_out_t, grads_ref, hid):
    e = bar.astype(BF16)
    a1 = (mm(w_out_t[...], e) * slope(h1)).astype(BF16)
    a0 = (mm(w_mid_t[...], a1) * slope(h0)).astype(BF16)
    grads_ref[:hid] += outer(a1, h0)
    grads_ref[hid : hid + R] += outer(inputs, a0)
    grads_ref[hid + R : hid + 2 * R] += outer(e, h1)
    return bar + mm(w_in_t[...], a0)


def span(i):
    return pl.ds(pl.multiple_of(i * CHUNK, CHUNK), CHUNK)


LANES = 128


def load_rows(dst, src):
    lines = dst.shape[1] // LANES
    dst[16:] = jnp.zeros((R - 16, dst.shape[1]), F32)
    for i in range(lines):
        dst[:Q, i * LANES : (i + 1) * LANES] = src[pl.ds(i, Q, stride=lines), :]


def store_lines(dst, first, value):
    lines = dst.shape[0] // Q
    for i in range(value.shape[1] // LANES):
        dst[pl.ds(first + i, Q, stride=lines), :] = value[:Q, i * LANES : (i + 1) * LANES]


def one_hot_layers(level, quadrant, pick):
    half = S // 2
    target = lax.broadcasted_iota(jnp.int32, (A, A), 1)
    source = lax.broadcasted_iota(jnp.int32, (A, A), 0)
    row, col = target // S, target % S
    fine = row // 2 * S + col // 2
    for face in range(6):
        q = quadrant[0, 0, face]
        high, low = q // 2, q % 2
        if face >= 4:
            high, low = low, high
        corner = high * half * S + low * half
        wanted = jnp.where(level[0, 0, face] == 1, corner + fine, target)
        pick[face] = jnp.where(source == wanted, 1.0, 0.0).astype(BF16)


def padded_rows(src, tall, flat, flipped):
    tall[...] = jnp.zeros(tall.shape, F32)
    tall[:Q] = src[...].astype(F32)
    flat[...] = tall[...].astype(BF16)
    flipped[...] = tall[...].T.astype(BF16)


def first_kernel(
    level, quadrant, table, pops, cot, w_in_rows, w_mid, w_out_rows,
    post, h_hbm, sheets, pick, w_in, w_in_t, w_out, w_out_t, wide, cot_wide, h_buf, tall, sems,
):
    g = Geometry(table)
    cells = wide.shape[1]
    load_rows(wide, pops)
    load_rows(cot_wide, cot)
    padded_rows(w_in_rows, tall, w_in_t, w_in)
    padded_rows(w_out_rows, tall, w_out, w_out_t)
    one_hot_layers(level, quadrant, pick)
    sheets[...] = jnp.zeros(sheets.shape, F32)

    def moved(i, j):
        return pltpu.make_async_copy(h_buf.at[j, :, span(i)], h_hbm.at[j, :, span(i)], sems.at[j, i])

    @pl.loop(0, cells // CHUNK)
    def _(i):
        at = span(i)
        _, h0, h1, out = collide(wide[:, at], w_in, w_mid, w_out)
        post[:, at] = out
        h_buf[0, :, at] = h0
        h_buf[1, :, at] = h1
        moved(i, 0).start()
        moved(i, 1).start()

    gather_sheets(g, post, sheets)
    gather_bars(g, cot_wide, pick, sheets)

    @pl.loop(0, cells // CHUNK)
    def _(i):
        moved(i, 0).wait()
        moved(i, 1).wait()


def middle_kernel(
    blocks, source, table, pick, recv, post1, cot, w_in, w_mid, w_out, w_in_t, w_mid_t, w_out_t,
    post2, bar, sheets, grads, state, wide, work, pbar, tmp,
):
    g = Geometry(table)
    cells = post1.shape[1]
    hid = w_mid.shape[0]
    slots = [slot_of(source, blocks, face) for face in (0, 1)]
    load_rows(wide, cot)
    stream(g, post1, recv, slots, pick, tmp, functools.partial(put, state))
    stream_back(g, wide, recv, slots, tmp, work, pbar)
    grads[...] = jnp.zeros(grads.shape, F32)
    sheets[...] = jnp.zeros(sheets.shape, F32)

    @pl.loop(0, cells // CHUNK)
    def _(i):
        at = span(i)
        inputs, h0, h1, out = collide(state[:, at], w_in, w_mid, w_out)
        post2[:, at] = out
        bar[:, at] = collide_back(pbar[:, at], inputs, h0, h1, w_in_t, w_mid_t, w_out_t, grads, hid)

    gather_sheets(g, post2, sheets)
    gather_bars(g, bar, pick, sheets)


def last_kernel(
    blocks, source, table, pick, recv, post2, bar, pops, h_hbm, grads_in, w_in_t, w_mid_t, w_out_t,
    final, grad_pops, grads, wide, work, pbar, tmp, h_buf, sems,
):
    g = Geometry(table)
    cells = post2.shape[1]
    hid = w_mid_t.shape[0]

    def moved(i, j):
        return pltpu.make_async_copy(h_hbm.at[j, :, span(i)], h_buf.at[j, :, span(i)], sems.at[j, i])

    @pl.loop(0, cells // CHUNK)
    def _(i):
        moved(i, 0).start()
        moved(i, 1).start()

    slots = [slot_of(source, blocks, face) for face in (0, 1)]
    load_rows(wide, pops)
    stream(g, post2, recv, slots, pick, tmp, lambda k, value: store_lines(final, k * A // LANES, value))
    stream_back(g, bar, recv, slots, tmp, work, pbar)
    grads[...] = grads_in[...]

    @pl.loop(0, cells // CHUNK)
    def _(i):
        at = span(i)
        moved(i, 0).wait()
        moved(i, 1).wait()
        out = collide_back(
            pbar[:, at], wide[:, at].astype(BF16), h_buf[0, :, at], h_buf[1, :, at],
            w_in_t, w_mid_t, w_out_t, grads, hid,
        )
        pbar[:, at] = out

    store_lines(grad_pops, 0, pbar[...])


OFFSETS = [d for d in range(-REACH, REACH + 1) if d != 0]


def exchange_kernel(blocks, slabs, sheets, recv, send_sem, recv_sem):
    me, level = lax.axis_index("blocks"), lax.axis_index("slab")
    side = [lax.rem(me - d + blocks, blocks) for d in OFFSETS]
    other = me + 1 - 2 * lax.rem(me, 2)
    above, below = lax.rem(level + 1, slabs), lax.rem(level + slabs - 1, slabs)
    barrier = pltpu.get_barrier_semaphore()
    for target in side:
        pl.semaphore_signal(barrier, inc=1, device_id={"blocks": target}, device_id_type=MESH)
    for target in (above, below):
        pl.semaphore_signal(barrier, inc=1, device_id={"slab": target}, device_id_type=MESH)
    pl.semaphore_wait(barrier, len(side) + 2)
    plan = [(0, i, {"blocks": target}) for i, target in enumerate(side)]
    plan.append((1, len(side), {"blocks": other}))
    plan.append((2, len(side) + 1, {"slab": below}))
    plan.append((2, len(side) + 2, {"slab": above}))
    copies = []
    for which, slot, device in plan:
        copy = pltpu.make_async_remote_copy(
            src_ref=sheets.at[which], dst_ref=recv.at[slot],
            send_sem=send_sem.at[slot], recv_sem=recv_sem.at[slot],
            device_id=device, device_id_type=MESH,
        )
        copy.start()
        copies.append(copy)
    for copy in copies:
        copy.wait()


PIECES = 3


def sum_kernel(chips, slabs, grads, out, land_c, half, land_t, part, land_s, sems):
    me, level = lax.axis_index("blocks"), lax.axis_index("slab")
    core, chip = lax.rem(me, 2), me // 2
    rows, width = part.shape[1], land_s.shape[-1]
    peer_t = [lax.rem(chip + d, chips) for d in range(1, chips)]
    peer_s = [lax.rem(level + d, slabs) for d in range(1, slabs)]
    twin = {"blocks": me + 1 - 2 * core}
    sides = [{"blocks": 2 * t + core} for t in peer_t]
    stack = [{"slab": t} for t in peer_s]
    barrier = pltpu.get_barrier_semaphore()
    for device in [twin] + sides + stack:
        pl.semaphore_signal(barrier, inc=1, device_id=device, device_id_type=MESH)
    pl.semaphore_wait(barrier, 1 + len(sides) + len(stack))

    def send(src, dst, p, which, device):
        copy = pltpu.make_async_remote_copy(
            src_ref=src, dst_ref=dst, send_sem=sems.at[0, p, which], recv_sem=sems.at[1, p, which],
            device_id=device, device_id_type=MESH,
        )
        copy.start()
        return copy

    def half_of(p, c):
        return pl.ds(pl.multiple_of((2 * p + c) * chips * rows, 8), chips * rows)

    def row_of(p):
        return pl.ds(pl.multiple_of(((2 * p + core) * chips + chip) * rows, 8), rows)

    def lane_of(i):
        return pl.ds(pl.multiple_of(i * width, 128), width)

    first_t, first_s = 1, len(sides) + 1
    again = len(sides) + len(stack) + 1
    flying = [[] for _ in range(PIECES)]

    def stage(p, number):
        for copy in flying[p]:
            copy.wait()
        if number == 0:
            flying[p] = [send(grads.at[half_of(p, 1 - core)], land_c.at[p], p, 0, twin)]
        if number == 1:
            half[p] = grads[half_of(p, core)] + land_c[p]
            flying[p] = [
                send(half.at[p, pl.ds(pl.multiple_of(t * rows, 8), rows)], land_t.at[p, i], p, first_t + i, device)
                for i, (t, device) in enumerate(zip(peer_t, sides))
            ]
        if number == 2:
            total = half[p, pl.ds(pl.multiple_of(chip * rows, 8), rows)]
            for i in range(len(sides)):
                total += land_t[p, i]
            part[p] = total
            flying[p] = [
                send(part.at[p, :, lane_of(t)], land_s.at[p, i], p, first_s + i, device)
                for i, (t, device) in enumerate(zip(peer_s, stack))
            ]
        if number == 3:
            mine = part[p, :, lane_of(level)]
            for i in range(len(stack)):
                mine += land_s[p, i]
            out[row_of(p), lane_of(level)] = mine
            spot = out.at[row_of(p), lane_of(level)]
            flying[p] = [send(spot, spot, p, again + first_s + i, device) for i, device in enumerate(stack)]
        if number == 4:
            spot = out.at[row_of(p)]
            flying[p] = [send(spot, spot, p, again + first_t + i, device) for i, device in enumerate(sides)]
        if number == 5:
            spot = out.at[half_of(p, core)]
            flying[p] = [send(spot, spot, p, again, twin)]

    for tick in range(6 + PIECES):
        for p in range(PIECES):
            if 0 <= tick - p <= 6:
                stage(p, tick - p)


def vmem(count):
    return [pl.BlockSpec(memory_space=pltpu.VMEM)] * count


SMEM_SPEC = pl.BlockSpec(memory_space=pltpu.SMEM)
ANY_SPEC = pl.BlockSpec(memory_space=pl.ANY)
LIMIT = 60 * 1024 * 1024


def shape(dims, dtype=F32):
    return jax.ShapeDtypeStruct(dims, dtype)


def shards(blocks, slabs, populations, w_in, w_mid, w_out, cotangent, face_source, face_level, face_quadrant):
    cells = populations.shape[-1]
    hid = w_in.shape[0]
    pops, cot = (v.reshape(Q * cells // LANES, LANES) for v in (populations, cotangent))
    table = jnp.asarray(row_table())
    w_mid = w_mid[0]
    w_mid_t = w_mid.T
    step = 8 * blocks * PIECES
    total_rows = -(-(hid + 2 * R) // step) * step
    parts = cells // CHUNK
    volume = pltpu.VMEM((R, cells), F32)
    tmp = pltpu.VMEM((R, A), F32)
    sheet_rows = 24
    params = pltpu.CompilerParams(vmem_limit_bytes=LIMIT)

    def exchange(sheets, which):
        count = 2 * REACH + 3
        return pl.pallas_call(
            functools.partial(exchange_kernel, blocks, slabs),
            out_shape=shape((count, sheet_rows, A)),
            in_specs=vmem(1),
            out_specs=vmem(1)[0],
            scratch_shapes=[pltpu.SemaphoreType.DMA((count,)), pltpu.SemaphoreType.DMA((count,))],
            compiler_params=pltpu.CompilerParams(collective_id=which, has_side_effects=True),
            name=f"exchange{which}",
        )(sheets)

    post1, hidden, sheets, pick, w_in, w_in_t, w_out, w_out_t = pl.pallas_call(
        first_kernel,
        out_shape=(
            shape((R, cells)), shape((2, hid, cells), BF16), shape((3, sheet_rows, A)), shape((6, A, A), BF16),
            shape((hid, R), BF16), shape((R, hid), BF16), shape((R, hid), BF16), shape((hid, R), BF16),
        ),
        in_specs=[SMEM_SPEC] * 2 + vmem(6),
        out_specs=(vmem(1)[0], ANY_SPEC, *vmem(6)),
        scratch_shapes=[
            volume, volume, pltpu.VMEM((2, hid, cells), BF16), pltpu.VMEM((R, hid), F32),
            pltpu.SemaphoreType.DMA((2, parts)),
        ],
        compiler_params=params,
        name="first",
    )(face_level, face_quadrant, table, pops, cot, w_in.T, w_mid, w_out)
    backs = (w_in_t, w_mid_t, w_out_t)
    recv = exchange(sheets, 0)
    post2, bar, sheets, grads = pl.pallas_call(
        functools.partial(middle_kernel, blocks),
        out_shape=(shape((R, cells)), shape((R, cells)), shape((3, sheet_rows, A)), shape((total_rows, hid))),
        in_specs=[SMEM_SPEC] + vmem(11),
        out_specs=tuple(vmem(4)),
        scratch_shapes=[volume] * 4 + [tmp],
        compiler_params=params,
        name="middle",
    )(face_source, table, pick, recv, post1, cot, w_in, w_mid, w_out, *backs)
    recv = exchange(sheets, 1)
    final, grad_pops, grads = pl.pallas_call(
        functools.partial(last_kernel, blocks),
        out_shape=(shape(pops.shape), shape(pops.shape), shape((total_rows, hid))),
        in_specs=[SMEM_SPEC] + vmem(6) + [ANY_SPEC] + vmem(4),
        out_specs=tuple(vmem(3)),
        scratch_shapes=[volume] * 3 + [tmp, pltpu.VMEM((2, hid, cells), BF16), pltpu.SemaphoreType.DMA((2, parts))],
        compiler_params=params,
        name="last",
    )(face_source, table, pick, recv, post2, bar, pops, hidden, grads, *backs)
    chips = blocks // 2
    rows, width = total_rows // (blocks * PIECES), hid // slabs
    total = pl.pallas_call(
        functools.partial(sum_kernel, chips, slabs),
        out_shape=shape((total_rows, hid)),
        in_specs=vmem(1),
        out_specs=vmem(1)[0],
        scratch_shapes=[
            pltpu.VMEM((PIECES, chips * rows, hid), F32),
            pltpu.VMEM((PIECES, chips * rows, hid), F32),
            pltpu.VMEM((PIECES, chips - 1, rows, hid), F32),
            pltpu.VMEM((PIECES, rows, hid), F32),
            pltpu.VMEM((PIECES, slabs - 1, rows, width), F32),
            pltpu.SemaphoreType.DMA((2, PIECES, 2 * (chips + slabs - 1))),
        ],
        compiler_params=pltpu.CompilerParams(collective_id=2, has_side_effects=True),
        name="sum_all",
    )(grads)
    total = total * float(blocks * slabs * cells) ** (-0.5)
    return (
        final.reshape(populations.shape),
        grad_pops.reshape(populations.shape),
        total[hid : hid + Q].T,
        total[:hid][None],
        total[hid + R : hid + R + Q],
    )


def solution(mesh):
    spread = P(None, "slab", "blocks", None)
    in_specs = (spread, P(), P(), P(), spread, P(), P("slab", "blocks", None), P("slab", "blocks", None))
    out_specs = (spread, spread, P(), P(), P())
    body = functools.partial(shards, mesh.shape["blocks"], mesh.shape["slab"])
    return jax.shard_map(body, mesh=mesh, in_specs=in_specs, out_specs=out_specs, check_vma=False)
```

```python
import functools

import jax
import jax.numpy as jnp
import numpy as np
from jax import lax
from jax.experimental import pallas as pl
from jax.experimental.pallas import tpu as pltpu
from jax.sharding import PartitionSpec as P

REACH = 3
R = 24
S = 16
A = S * S
CHUNK = 1024
MESH = pl.DeviceIdType.MESH
F32, BF16 = jnp.float32, jnp.bfloat16

VELOCITIES = [
    (0, 0, 0),
    (1, 0, 0),
    (-1, 0, 0),
    (0, 1, 0),
    (0, -1, 0),
    (0, 0, 1),
    (0, 0, -1),
    (1, 1, 0),
    (-1, -1, 0),
    (1, -1, 0),
    (-1, 1, 0),
    (1, 0, 1),
    (-1, 0, -1),
    (1, 0, -1),
    (-1, 0, 1),
    (0, 1, 1),
    (0, -1, -1),
    (0, 1, -1),
    (0, -1, 1),
]
Q = len(VELOCITIES)


def row_table():
    table = np.zeros((4, R, A), np.int32)
    for q, v in enumerate(VELOCITIES):
        for axis in range(3):
            table[axis, q] = v[axis]
        if q:
            table[3, q] = 1 if q % 2 else -1
    return table


def lane_roll(x, shift):
    shift %= A
    return x if shift == 0 else pltpu.roll(x, shift, 1)


class Geometry:
    def __init__(self, table_ref):
        lane = lax.broadcasted_iota(jnp.int32, (R, A), 1)
        y, z = lane // S, lane % S
        self.v = [table_ref[axis] for axis in range(3)]
        self.plus = [v == 1 for v in self.v]
        self.minus = [v == -1 for v in self.v]
        parity = table_ref[3]
        self.odd, self.even = parity == 1, parity == -1
        py, my, pz, mz = self.plus[1], self.minus[1], self.plus[2], self.minus[2]
        self.ly = (py & (y == 0)) | (my & (y == S - 1))
        self.lz = (pz & (z == 0)) | (mz & (z == S - 1))
        self.oy = (py & (y == S - 1)) | (my & (y == 0))
        self.oz = (pz & (z == S - 1)) | (mz & (z == 0))

    def row_roll(self, x, axis, step, sign=1):
        up, down = lane_roll(x, sign * step), lane_roll(x, -sign * step)
        return jnp.where(self.plus[axis], up, jnp.where(self.minus[axis], down, x))

    def opposite(self, x):
        return jnp.where(self.odd, pltpu.roll(x, R - 1, 0), jnp.where(self.even, pltpu.roll(x, 1, 0), x))

    def leaving_x(self, k):
        if k == 0:
            return self.plus[0]
        if k == S - 1:
            return self.minus[0]
        return None

    def crossings(self, k):
        ly, lz, lx = self.ly, self.lz, self.leaving_x(k)
        two, some = ly & lz, ly | lz
        if lx is None:
            return ly & ~lz, lz & ~ly, None, two, ~some
        return (
            ly & ~lz & ~lx,
            lz & ~ly & ~lx,
            lx & ~some,
            two | (lx & some),
            ~(some | lx),
        )


def layer(ref, k):
    return ref[:, k * A : (k + 1) * A]


def put(ref, k, value):
    ref[:, k * A : (k + 1) * A] = value


def split3(x):
    hi = x.astype(BF16)
    rest = x - hi.astype(F32)
    mid = rest.astype(BF16)
    low = (rest - mid.astype(F32)).astype(BF16)
    return jnp.concatenate([hi, mid, low], axis=0)


def refine(g, sheet, axis, pick_ref, transposed):
    parts = split3(sheet)
    dims = (((1,), (1 if transposed else 0,)), ((), ()))
    both = []
    for face in (2 * axis, 2 * axis + 1):
        r = lax.dot_general(parts, pick_ref[face], dims, preferred_element_type=F32)
        both.append(r[:R] + r[R : 2 * R] + r[2 * R :])
    return jnp.where(g.minus[axis], both[0], both[1])


PACK = [
    [(0, 1, 3), (2, 7, 15)],
    [(0, 3, 5), (2, 7, 11), (6, 15, 19)],
    [(0, 5, 7), (2, 11, 19)],
]
FACED = 10


def pack(sheets_ref, axis, base, value):
    for at, low, high in PACK[axis]:
        sheets_ref[axis, base + at : base + at + high - low] = value[low:high]


def unpack(recv_ref, slot, axis, base, tmp_ref):
    tmp_ref[...] = jnp.zeros(tmp_ref.shape, F32)
    for at, low, high in PACK[axis]:
        tmp_ref[low:high] = recv_ref[slot, base + at : base + at + high - low]
    return tmp_ref[...]


def slot_of(source_ref, blocks, face):
    me = lax.axis_index("blocks")
    distance = lax.rem(source_ref[face, me] - me + blocks, blocks)
    distance = jnp.where(distance > blocks // 2, distance - blocks, distance)
    slot = jnp.where(distance < 0, distance + REACH, distance + REACH - 1)
    return jnp.clip(slot, 0, 2 * REACH - 1)


def gather_sheets(g, ref, sheets_ref):
    acc_y = acc_z = None
    for k in range(S):
        a = layer(ref, k)
        ty = lane_roll(jnp.where(g.oy, a, 0.0), S * k)
        tz = lane_roll(jnp.where(g.oz, a, 0.0), k)
        acc_y = ty if acc_y is None else acc_y + ty
        acc_z = tz if acc_z is None else acc_z + tz
    sheet_x = jnp.where(g.plus[0], layer(ref, S - 1), jnp.where(g.minus[0], layer(ref, 0), 0.0))
    pack(sheets_ref, 0, 0, sheet_x)
    pack(sheets_ref, 1, 0, jnp.where(g.plus[1], lane_roll(acc_y, S), acc_y))
    pack(sheets_ref, 2, 0, jnp.where(g.plus[2], lane_roll(acc_z, -(S - 1)), acc_z))


def gather_bars(g, ref, pick_ref, sheets_ref):
    acc_x = acc_y = acc_z = None
    for k in range(S):
        b = layer(ref, k)
        one_y, one_z, one_x, _, _ = g.crossings(k)
        ty = lane_roll(jnp.where(one_y, b, 0.0), S * k)
        tz = lane_roll(jnp.where(one_z, b, 0.0), k)
        acc_y = ty if acc_y is None else acc_y + ty
        acc_z = tz if acc_z is None else acc_z + tz
        if one_x is not None:
            tx = jnp.where(one_x, b, 0.0)
            acc_x = tx if acc_x is None else acc_x + tx
    acc_y = jnp.where(g.minus[1], lane_roll(acc_y, S), acc_y)
    acc_z = jnp.where(g.minus[2], lane_roll(acc_z, -(S - 1)), acc_z)
    gx = g.row_roll(g.row_roll(acc_x, 1, S, -1), 2, 1, -1)
    gy = g.row_roll(g.row_roll(acc_y, 0, S, -1), 2, 1, -1)
    gz = g.row_roll(g.row_roll(acc_z, 1, S, -1), 0, 1, -1)
    for axis, value in enumerate((gx, gy, gz)):
        pack(sheets_ref, axis, FACED, refine(g, value, axis, pick_ref, True))


def received(g, recv_ref, slots, base, toward, tmp_ref):
    sides = [unpack(recv_ref, slot, 0, base, tmp_ref) for slot in slots]
    x = jnp.where(toward[0], sides[0], sides[1])
    y = unpack(recv_ref, 2 * REACH, 1, base, tmp_ref)
    sides = [unpack(recv_ref, 2 * REACH + side, 2, base, tmp_ref) for side in (1, 2)]
    return x, y, jnp.where(toward[2], sides[0], sides[1])


def stream(g, post_ref, recv_ref, slots, pick_ref, tmp_ref, store):
    raw_x, raw_y, raw_z = received(g, recv_ref, slots, 0, g.minus, tmp_ref)
    gx, gy, gz = (refine(g, raw, axis, pick_ref, False) for axis, raw in enumerate((raw_x, raw_y, raw_z)))
    sx = g.row_roll(g.row_roll(gx, 1, S), 2, 1)
    sy = g.row_roll(g.row_roll(gy, 0, S), 2, 1)
    sz = g.row_roll(g.row_roll(gz, 1, S), 0, 1)
    sy = jnp.where(g.minus[1], lane_roll(sy, -S), sy)
    sz = jnp.where(g.minus[2], lane_roll(sz, S - 1), sz)
    for k in range(S):
        here = layer(post_ref, k)
        behind = layer(post_ref, max(k - 1, 0))
        ahead = layer(post_ref, min(k + 1, S - 1))
        moved = jnp.where(g.plus[0], behind, jnp.where(g.minus[0], ahead, here))
        moved = g.row_roll(g.row_roll(moved, 1, S), 2, 1)
        one_y, one_z, one_x, two, _ = g.crossings(k)
        out = jnp.where(one_y, lane_roll(sy, -S * k), moved)
        out = jnp.where(one_z, lane_roll(sz, -k), out)
        if one_x is not None:
            out = jnp.where(one_x, sx, out)
        out = jnp.where(two, g.opposite(here), out)
        store(k, out)


def stream_back(g, bar_ref, recv_ref, slots, tmp_ref, work_ref, out_ref):
    ox, oy, oz = received(g, recv_ref, slots, FACED, g.plus, tmp_ref)
    oy = jnp.where(g.plus[1], lane_roll(oy, -S), oy)
    oz = jnp.where(g.plus[2], lane_roll(oz, S - 1), oz)
    for k in range(S):
        put(work_ref, k, jnp.where(g.crossings(k)[4], layer(bar_ref, k), 0.0))
    for k in range(S):
        zero = jnp.zeros((R, A), F32)
        ahead = layer(work_ref, k + 1) if k + 1 < S else zero
        behind = layer(work_ref, k - 1) if k > 0 else zero
        moved = jnp.where(g.plus[0], ahead, jnp.where(g.minus[0], behind, layer(work_ref, k)))
        out = g.row_roll(g.row_roll(moved, 1, S, -1), 2, 1, -1)
        out += g.opposite(jnp.where(g.crossings(k)[3], layer(bar_ref, k), 0.0))
        out += jnp.where(g.oy, lane_roll(oy, -S * k), 0.0)
        out += jnp.where(g.oz, lane_roll(oz, -k), 0.0)
        if k == 0:
            out += jnp.where(g.minus[0], ox, 0.0)
        if k == S - 1:
            out += jnp.where(g.plus[0], ox, 0.0)
        put(out_ref, k, out)


def mm(a, b):
    return jnp.dot(a, b, preferred_element_type=F32)


def outer(a, b):
    return lax.dot_general(a, b, (((1,), (1,)), ((), ())), preferred_element_type=F32)


def slope(h):
    wide = h.astype(F32)
    return 1.0 - wide * wide


def collide(x, w_in, w_mid, w_out):
    inputs = x.astype(BF16)
    h0 = jnp.tanh(mm(w_in[...], inputs)).astype(BF16)
    h1 = jnp.tanh(mm(w_mid[...], h0)).astype(BF16)
    return inputs, h0, h1, x + mm(w_out[...], h1)


def collide_back(bar, inputs, h0, h1, w_in_t, w_mid_t, w_out_t, grads_ref, hid):
    e = bar.astype(BF16)
    a1 = (mm(w_out_t[...], e) * slope(h1)).astype(BF16)
    a0 = (mm(w_mid_t[...], a1) * slope(h0)).astype(BF16)
    grads_ref[:hid] += outer(a1, h0)
    grads_ref[hid : hid + R] += outer(inputs, a0)
    grads_ref[hid + R : hid + 2 * R] += outer(e, h1)
    return bar + mm(w_in_t[...], a0)


def span(i):
    return pl.ds(pl.multiple_of(i * CHUNK, CHUNK), CHUNK)


LANES = 128


def load_rows(dst, src):
    lines = dst.shape[1] // LANES
    dst[16:] = jnp.zeros((R - 16, dst.shape[1]), F32)
    for i in range(lines):
        dst[:Q, i * LANES : (i + 1) * LANES] = src[pl.ds(i, Q, stride=lines), :]


def store_lines(dst, first, value):
    lines = dst.shape[0] // Q
    for i in range(value.shape[1] // LANES):
        dst[pl.ds(first + i, Q, stride=lines), :] = value[:Q, i * LANES : (i + 1) * LANES]


def one_hot_layers(level, quadrant, pick):
    half = S // 2
    target = lax.broadcasted_iota(jnp.int32, (A, A), 1)
    source = lax.broadcasted_iota(jnp.int32, (A, A), 0)
    row, col = target // S, target % S
    fine = row // 2 * S + col // 2
    for face in range(6):
        q = quadrant[0, 0, face]
        high, low = q // 2, q % 2
        if face >= 4:
            high, low = low, high
        corner = high * half * S + low * half
        wanted = jnp.where(level[0, 0, face] == 1, corner + fine, target)
        pick[face] = jnp.where(source == wanted, 1.0, 0.0).astype(BF16)


def padded_rows(src, tall, flat, flipped):
    tall[...] = jnp.zeros(tall.shape, F32)
    tall[:Q] = src[...].astype(F32)
    flat[...] = tall[...].astype(BF16)
    flipped[...] = tall[...].T.astype(BF16)


def first_kernel(
    level, quadrant, table, pops, cot, w_in_rows, w_mid, w_out_rows,
    post, h_hbm, sheets, pick, w_in, w_in_t, w_out, w_out_t, w_mid_t, wide, cot_wide, h_buf, tall, sems,
):
    g = Geometry(table)
    cells = wide.shape[1]
    load_rows(wide, pops)
    load_rows(cot_wide, cot)
    padded_rows(w_in_rows, tall, w_in_t, w_in)
    padded_rows(w_out_rows, tall, w_out, w_out_t)
    w_mid_t[...] = w_mid[...].astype(F32).T.astype(BF16)
    one_hot_layers(level, quadrant, pick)
    sheets[...] = jnp.zeros(sheets.shape, F32)

    def moved(i, j):
        return pltpu.make_async_copy(h_buf.at[j, :, span(i)], h_hbm.at[j, :, span(i)], sems.at[j, i])

    @pl.loop(0, cells // CHUNK)
    def _(i):
        at = span(i)
        _, h0, h1, out = collide(wide[:, at], w_in, w_mid, w_out)
        post[:, at] = out
        h_buf[0, :, at] = h0
        h_buf[1, :, at] = h1
        moved(i, 0).start()
        moved(i, 1).start()

    gather_sheets(g, post, sheets)
    gather_bars(g, cot_wide, pick, sheets)

    @pl.loop(0, cells // CHUNK)
    def _(i):
        moved(i, 0).wait()
        moved(i, 1).wait()


def middle_kernel(
    blocks, source, table, pick, recv, post1, cot, w_in, w_mid, w_out, w_in_t, w_mid_t, w_out_t,
    post2, bar, sheets, grads, state, wide, work, pbar, tmp,
):
    g = Geometry(table)
    cells = post1.shape[1]
    hid = w_mid.shape[0]
    slots = [slot_of(source, blocks, face) for face in (0, 1)]
    load_rows(wide, cot)
    stream(g, post1, recv, slots, pick, tmp, functools.partial(put, state))
    stream_back(g, wide, recv, slots, tmp, work, pbar)
    grads[...] = jnp.zeros(grads.shape, F32)
    sheets[...] = jnp.zeros(sheets.shape, F32)

    @pl.loop(0, cells // CHUNK)
    def _(i):
        at = span(i)
        inputs, h0, h1, out = collide(state[:, at], w_in, w_mid, w_out)
        post2[:, at] = out
        bar[:, at] = collide_back(pbar[:, at], inputs, h0, h1, w_in_t, w_mid_t, w_out_t, grads, hid)

    gather_sheets(g, post2, sheets)
    gather_bars(g, bar, pick, sheets)


def last_kernel(
    blocks, source, table, pick, recv, post2, bar, pops, h_hbm, grads_in, w_in_t, w_mid_t, w_out_t,
    final, grad_pops, grads, wide, work, pbar, tmp, h_buf, sems,
):
    g = Geometry(table)
    cells = post2.shape[1]
    hid = w_mid_t.shape[0]

    def moved(i, j):
        return pltpu.make_async_copy(h_hbm.at[j, :, span(i)], h_buf.at[j, :, span(i)], sems.at[j, i])

    @pl.loop(0, cells // CHUNK)
    def _(i):
        moved(i, 0).start()
        moved(i, 1).start()

    slots = [slot_of(source, blocks, face) for face in (0, 1)]
    load_rows(wide, pops)
    stream(g, post2, recv, slots, pick, tmp, lambda k, value: store_lines(final, k * A // LANES, value))
    stream_back(g, bar, recv, slots, tmp, work, pbar)
    grads[...] = grads_in[...]

    @pl.loop(0, cells // CHUNK)
    def _(i):
        at = span(i)
        moved(i, 0).wait()
        moved(i, 1).wait()
        out = collide_back(
            pbar[:, at], wide[:, at].astype(BF16), h_buf[0, :, at], h_buf[1, :, at],
            w_in_t, w_mid_t, w_out_t, grads, hid,
        )
        pbar[:, at] = out

    store_lines(grad_pops, 0, pbar[...])


OFFSETS = [d for d in range(-REACH, REACH + 1) if d != 0]


def exchange_kernel(blocks, slabs, sheets, recv, send_sem, recv_sem):
    me, level = lax.axis_index("blocks"), lax.axis_index("slab")
    side = [lax.rem(me - d + blocks, blocks) for d in OFFSETS]
    other = me + 1 - 2 * lax.rem(me, 2)
    above, below = lax.rem(level + 1, slabs), lax.rem(level + slabs - 1, slabs)
    barrier = pltpu.get_barrier_semaphore()
    for target in side:
        pl.semaphore_signal(barrier, inc=1, device_id={"blocks": target}, device_id_type=MESH)
    for target in (above, below):
        pl.semaphore_signal(barrier, inc=1, device_id={"slab": target}, device_id_type=MESH)
    pl.semaphore_wait(barrier, len(side) + 2)
    plan = [(0, i, {"blocks": target}) for i, target in enumerate(side)]
    plan.append((1, len(side), {"blocks": other}))
    plan.append((2, len(side) + 1, {"slab": below}))
    plan.append((2, len(side) + 2, {"slab": above}))
    copies = []
    for which, slot, device in plan:
        copy = pltpu.make_async_remote_copy(
            src_ref=sheets.at[which], dst_ref=recv.at[slot],
            send_sem=send_sem.at[slot], recv_sem=recv_sem.at[slot],
            device_id=device, device_id_type=MESH,
        )
        copy.start()
        copies.append(copy)
    for copy in copies:
        copy.wait()


PIECES = 3


def sum_kernel(chips, slabs, grads, out, land_c, half, land_t, part, land_s, sems):
    me, level = lax.axis_index("blocks"), lax.axis_index("slab")
    core, chip = lax.rem(me, 2), me // 2
    rows, width = part.shape[1], land_s.shape[-1]
    peer_t = [lax.rem(chip + d, chips) for d in range(1, chips)]
    peer_s = [lax.rem(level + d, slabs) for d in range(1, slabs)]
    twin = {"blocks": me + 1 - 2 * core}
    sides = [{"blocks": 2 * t + core} for t in peer_t]
    stack = [{"slab": t} for t in peer_s]
    barrier = pltpu.get_barrier_semaphore()
    for device in [twin] + sides + stack:
        pl.semaphore_signal(barrier, inc=1, device_id=device, device_id_type=MESH)
    pl.semaphore_wait(barrier, 1 + len(sides) + len(stack))

    def send(src, dst, p, which, device):
        copy = pltpu.make_async_remote_copy(
            src_ref=src, dst_ref=dst, send_sem=sems.at[0, p, which], recv_sem=sems.at[1, p, which],
            device_id=device, device_id_type=MESH,
        )
        copy.start()
        return copy

    def half_of(p, c):
        return pl.ds(pl.multiple_of((2 * p + c) * chips * rows, 8), chips * rows)

    def row_of(p):
        return pl.ds(pl.multiple_of(((2 * p + core) * chips + chip) * rows, 8), rows)

    def lane_of(i):
        return pl.ds(pl.multiple_of(i * width, 128), width)

    first_t, first_s = 1, len(sides) + 1
    again = len(sides) + len(stack) + 1
    flying = [[] for _ in range(PIECES)]

    def stage(p, number):
        for copy in flying[p]:
            copy.wait()
        if number == 0:
            flying[p] = [send(grads.at[half_of(p, 1 - core)], land_c.at[p], p, 0, twin)]
        if number == 1:
            half[p] = grads[half_of(p, core)] + land_c[p]
            flying[p] = [
                send(half.at[p, pl.ds(pl.multiple_of(t * rows, 8), rows)], land_t.at[p, i], p, first_t + i, device)
                for i, (t, device) in enumerate(zip(peer_t, sides))
            ]
        if number == 2:
            total = half[p, pl.ds(pl.multiple_of(chip * rows, 8), rows)]
            for i in range(len(sides)):
                total += land_t[p, i]
            part[p] = total
            flying[p] = [
                send(part.at[p, :, lane_of(t)], land_s.at[p, i], p, first_s + i, device)
                for i, (t, device) in enumerate(zip(peer_s, stack))
            ]
        if number == 3:
            mine = part[p, :, lane_of(level)]
            for i in range(len(stack)):
                mine += land_s[p, i]
            out[row_of(p), lane_of(level)] = mine
            spot = out.at[row_of(p), lane_of(level)]
            flying[p] = [send(spot, spot, p, again + first_s + i, device) for i, device in enumerate(stack)]
        if number == 4:
            spot = out.at[row_of(p)]
            flying[p] = [send(spot, spot, p, again + first_t + i, device) for i, device in enumerate(sides)]
        if number == 5:
            spot = out.at[half_of(p, core)]
            flying[p] = [send(spot, spot, p, again, twin)]

    for number in (0, 1):
        for p in range(PIECES):
            stage(p, number)
    for tick in range(2, 5 + PIECES + 2):
        for p in range(PIECES):
            number = tick - p
            if 2 <= number <= 6:
                stage(p, number)


def vmem(count):
    return [pl.BlockSpec(memory_space=pltpu.VMEM)] * count


SMEM_SPEC = pl.BlockSpec(memory_space=pltpu.SMEM)
ANY_SPEC = pl.BlockSpec(memory_space=pl.ANY)
LIMIT = 60 * 1024 * 1024


def shape(dims, dtype=F32):
    return jax.ShapeDtypeStruct(dims, dtype)


def shards(blocks, slabs, populations, w_in, w_mid, w_out, cotangent, face_source, face_level, face_quadrant):
    cells = populations.shape[-1]
    hid = w_in.shape[0]
    pops, cot = (v.reshape(Q * cells // LANES, LANES) for v in (populations, cotangent))
    table = jnp.asarray(row_table())
    w_mid = w_mid[0]
    step = 8 * blocks * PIECES
    total_rows = -(-(hid + 2 * R) // step) * step
    parts = cells // CHUNK
    volume = pltpu.VMEM((R, cells), F32)
    tmp = pltpu.VMEM((R, A), F32)
    sheet_rows = 24
    params = pltpu.CompilerParams(vmem_limit_bytes=LIMIT)

    def exchange(sheets, which):
        count = 2 * REACH + 3
        return pl.pallas_call(
            functools.partial(exchange_kernel, blocks, slabs),
            out_shape=shape((count, sheet_rows, A)),
            in_specs=vmem(1),
            out_specs=vmem(1)[0],
            scratch_shapes=[pltpu.SemaphoreType.DMA((count,)), pltpu.SemaphoreType.DMA((count,))],
            compiler_params=pltpu.CompilerParams(collective_id=which, has_side_effects=True),
            name=f"exchange{which}",
        )(sheets)

    post1, hidden, sheets, pick, w_in, w_in_t, w_out, w_out_t, w_mid_t = pl.pallas_call(
        first_kernel,
        out_shape=(
            shape((R, cells)), shape((2, hid, cells), BF16), shape((3, sheet_rows, A)), shape((6, A, A), BF16),
            shape((hid, R), BF16), shape((R, hid), BF16), shape((R, hid), BF16), shape((hid, R), BF16),
            shape((hid, hid), BF16),
        ),
        in_specs=[SMEM_SPEC] * 2 + vmem(6),
        out_specs=(vmem(1)[0], ANY_SPEC, *vmem(7)),
        scratch_shapes=[
            volume, volume, pltpu.VMEM((2, hid, cells), BF16), pltpu.VMEM((R, hid), F32),
            pltpu.SemaphoreType.DMA((2, parts)),
        ],
        compiler_params=params,
        name="first",
    )(face_level, face_quadrant, table, pops, cot, w_in.T, w_mid, w_out)
    backs = (w_in_t, w_mid_t, w_out_t)
    recv = exchange(sheets, 0)
    post2, bar, sheets, grads = pl.pallas_call(
        functools.partial(middle_kernel, blocks),
        out_shape=(shape((R, cells)), shape((R, cells)), shape((3, sheet_rows, A)), shape((total_rows, hid))),
        in_specs=[SMEM_SPEC] + vmem(11),
        out_specs=tuple(vmem(4)),
        scratch_shapes=[volume] * 4 + [tmp],
        compiler_params=params,
        name="middle",
    )(face_source.T, table, pick, recv, post1, cot, w_in, w_mid, w_out, *backs)
    recv = exchange(sheets, 1)
    final, grad_pops, grads = pl.pallas_call(
        functools.partial(last_kernel, blocks),
        out_shape=(shape(pops.shape), shape(pops.shape), shape((total_rows, hid))),
        in_specs=[SMEM_SPEC] + vmem(6) + [ANY_SPEC] + vmem(4),
        out_specs=tuple(vmem(3)),
        scratch_shapes=[volume] * 3 + [tmp, pltpu.VMEM((2, hid, cells), BF16), pltpu.SemaphoreType.DMA((2, parts))],
        compiler_params=params,
        name="last",
    )(face_source.T, table, pick, recv, post2, bar, pops, hidden, grads, *backs)
    chips = blocks // 2
    rows, width = total_rows // (blocks * PIECES), hid // slabs
    total = pl.pallas_call(
        functools.partial(sum_kernel, chips, slabs),
        out_shape=shape((total_rows, hid)),
        in_specs=vmem(1),
        out_specs=vmem(1)[0],
        scratch_shapes=[
            pltpu.VMEM((PIECES, chips * rows, hid), F32),
            pltpu.VMEM((PIECES, chips * rows, hid), F32),
            pltpu.VMEM((PIECES, chips - 1, rows, hid), F32),
            pltpu.VMEM((PIECES, rows, hid), F32),
            pltpu.VMEM((PIECES, slabs - 1, rows, width), F32),
            pltpu.SemaphoreType.DMA((2, PIECES, 2 * (chips + slabs - 1))),
        ],
        compiler_params=pltpu.CompilerParams(collective_id=2, has_side_effects=True),
        name="sum_all",
    )(grads)
    total = total * float(blocks * slabs * cells) ** (-0.5)
    return (
        final.reshape(populations.shape),
        grad_pops.reshape(populations.shape),
        total[hid : hid + Q].T,
        total[:hid][None],
        total[hid + R : hid + R + Q],
    )


def solution(mesh):
    spread = P(None, "slab", "blocks", None)
    in_specs = (spread, P(), P(), P(), spread, P(), P("slab", "blocks", None), P("slab", "blocks", None))
    out_specs = (spread, spread, P(), P(), P())
    body = functools.partial(shards, mesh.shape["blocks"], mesh.shape["slab"])
    return jax.shard_map(body, mesh=mesh, in_specs=in_specs, out_specs=out_specs, check_vma=False)
```

```python
import functools

import jax
import jax.numpy as jnp
import numpy as np
from jax import lax
from jax.experimental import pallas as pl
from jax.experimental.pallas import tpu as pltpu
from jax.sharding import PartitionSpec as P

REACH = 3
R = 24
S = 16
A = S * S
CHUNK = 1024
MESH = pl.DeviceIdType.MESH
F32, BF16 = jnp.float32, jnp.bfloat16

VELOCITIES = [
    (0, 0, 0),
    (1, 0, 0),
    (-1, 0, 0),
    (0, 1, 0),
    (0, -1, 0),
    (0, 0, 1),
    (0, 0, -1),
    (1, 1, 0),
    (-1, -1, 0),
    (1, -1, 0),
    (-1, 1, 0),
    (1, 0, 1),
    (-1, 0, -1),
    (1, 0, -1),
    (-1, 0, 1),
    (0, 1, 1),
    (0, -1, -1),
    (0, 1, -1),
    (0, -1, 1),
]
Q = len(VELOCITIES)


def row_table():
    table = np.zeros((4, R, A), np.int32)
    for q, v in enumerate(VELOCITIES):
        for axis in range(3):
            table[axis, q] = v[axis]
        if q:
            table[3, q] = 1 if q % 2 else -1
    return table


def lane_roll(x, shift):
    shift %= A
    return x if shift == 0 else pltpu.roll(x, shift, 1)


class Geometry:
    def __init__(self, table_ref):
        lane = lax.broadcasted_iota(jnp.int32, (R, A), 1)
        y, z = lane // S, lane % S
        self.v = [table_ref[axis] for axis in range(3)]
        self.plus = [v == 1 for v in self.v]
        self.minus = [v == -1 for v in self.v]
        parity = table_ref[3]
        self.odd, self.even = parity == 1, parity == -1
        py, my, pz, mz = self.plus[1], self.minus[1], self.plus[2], self.minus[2]
        self.ly = (py & (y == 0)) | (my & (y == S - 1))
        self.lz = (pz & (z == 0)) | (mz & (z == S - 1))
        self.oy = (py & (y == S - 1)) | (my & (y == 0))
        self.oz = (pz & (z == S - 1)) | (mz & (z == 0))

    def row_roll(self, x, axis, step, sign=1):
        up, down = lane_roll(x, sign * step), lane_roll(x, -sign * step)
        return jnp.where(self.plus[axis], up, jnp.where(self.minus[axis], down, x))

    def opposite(self, x):
        return jnp.where(self.odd, pltpu.roll(x, R - 1, 0), jnp.where(self.even, pltpu.roll(x, 1, 0), x))

    def leaving_x(self, k):
        if k == 0:
            return self.plus[0]
        if k == S - 1:
            return self.minus[0]
        return None

    def crossings(self, k):
        ly, lz, lx = self.ly, self.lz, self.leaving_x(k)
        two, some = ly & lz, ly | lz
        if lx is None:
            return ly & ~lz, lz & ~ly, None, two, ~some
        return (
            ly & ~lz & ~lx,
            lz & ~ly & ~lx,
            lx & ~some,
            two | (lx & some),
            ~(some | lx),
        )


def layer(ref, k):
    return ref[:, k * A : (k + 1) * A]


def put(ref, k, value):
    ref[:, k * A : (k + 1) * A] = value


def split3(x):
    hi = x.astype(BF16)
    rest = x - hi.astype(F32)
    mid = rest.astype(BF16)
    low = (rest - mid.astype(F32)).astype(BF16)
    return jnp.concatenate([hi, mid, low], axis=0)


def refine(g, sheet, axis, pick_ref, transposed):
    parts = split3(sheet)
    dims = (((1,), (1 if transposed else 0,)), ((), ()))
    both = []
    for face in (2 * axis, 2 * axis + 1):
        r = lax.dot_general(parts, pick_ref[face], dims, preferred_element_type=F32)
        both.append(r[:R] + r[R : 2 * R] + r[2 * R :])
    return jnp.where(g.minus[axis], both[0], both[1])


PACK = [
    [(0, 1, 3), (2, 7, 15)],
    [(0, 3, 5), (2, 7, 11), (6, 15, 19)],
    [(0, 5, 7), (2, 11, 19)],
]
FACED = 10


def pack(sheets_ref, axis, base, value):
    for at, low, high in PACK[axis]:
        sheets_ref[axis, base + at : base + at + high - low] = value[low:high]


def unpack(recv_ref, slot, axis, base, tmp_ref):
    tmp_ref[...] = jnp.zeros(tmp_ref.shape, F32)
    for at, low, high in PACK[axis]:
        tmp_ref[low:high] = recv_ref[slot, base + at : base + at + high - low]
    return tmp_ref[...]


def slot_of(source_ref, blocks, face):
    me = lax.axis_index("blocks")
    distance = lax.rem(source_ref[face, me] - me + blocks, blocks)
    distance = jnp.where(distance > blocks // 2, distance - blocks, distance)
    slot = jnp.where(distance < 0, distance + REACH, distance + REACH - 1)
    return jnp.clip(slot, 0, 2 * REACH - 1)


def gather_sheets(g, ref, sheets_ref):
    acc_y = acc_z = None
    for k in range(S):
        a = layer(ref, k)
        ty = lane_roll(jnp.where(g.oy, a, 0.0), S * k)
        tz = lane_roll(jnp.where(g.oz, a, 0.0), k)
        acc_y = ty if acc_y is None else acc_y + ty
        acc_z = tz if acc_z is None else acc_z + tz
    sheet_x = jnp.where(g.plus[0], layer(ref, S - 1), jnp.where(g.minus[0], layer(ref, 0), 0.0))
    pack(sheets_ref, 0, 0, sheet_x)
    pack(sheets_ref, 1, 0, jnp.where(g.plus[1], lane_roll(acc_y, S), acc_y))
    pack(sheets_ref, 2, 0, jnp.where(g.plus[2], lane_roll(acc_z, -(S - 1)), acc_z))


def gather_bars(g, ref, pick_ref, sheets_ref):
    acc_x = acc_y = acc_z = None
    for k in range(S):
        b = layer(ref, k)
        one_y, one_z, one_x, _, _ = g.crossings(k)
        ty = lane_roll(jnp.where(one_y, b, 0.0), S * k)
        tz = lane_roll(jnp.where(one_z, b, 0.0), k)
        acc_y = ty if acc_y is None else acc_y + ty
        acc_z = tz if acc_z is None else acc_z + tz
        if one_x is not None:
            tx = jnp.where(one_x, b, 0.0)
            acc_x = tx if acc_x is None else acc_x + tx
    acc_y = jnp.where(g.minus[1], lane_roll(acc_y, S), acc_y)
    acc_z = jnp.where(g.minus[2], lane_roll(acc_z, -(S - 1)), acc_z)
    gx = g.row_roll(g.row_roll(acc_x, 1, S, -1), 2, 1, -1)
    gy = g.row_roll(g.row_roll(acc_y, 0, S, -1), 2, 1, -1)
    gz = g.row_roll(g.row_roll(acc_z, 1, S, -1), 0, 1, -1)
    for axis, value in enumerate((gx, gy, gz)):
        pack(sheets_ref, axis, FACED, refine(g, value, axis, pick_ref, True))


def received(g, recv_ref, slots, base, toward, tmp_ref):
    sides = [unpack(recv_ref, slot, 0, base, tmp_ref) for slot in slots]
    x = jnp.where(toward[0], sides[0], sides[1])
    y = unpack(recv_ref, 2 * REACH, 1, base, tmp_ref)
    sides = [unpack(recv_ref, 2 * REACH + side, 2, base, tmp_ref) for side in (1, 2)]
    return x, y, jnp.where(toward[2], sides[0], sides[1])


def stream(g, post_ref, recv_ref, slots, pick_ref, tmp_ref, store):
    raw_x, raw_y, raw_z = received(g, recv_ref, slots, 0, g.minus, tmp_ref)
    gx, gy, gz = (refine(g, raw, axis, pick_ref, False) for axis, raw in enumerate((raw_x, raw_y, raw_z)))
    sx = g.row_roll(g.row_roll(gx, 1, S), 2, 1)
    sy = g.row_roll(g.row_roll(gy, 0, S), 2, 1)
    sz = g.row_roll(g.row_roll(gz, 1, S), 0, 1)
    sy = jnp.where(g.minus[1], lane_roll(sy, -S), sy)
    sz = jnp.where(g.minus[2], lane_roll(sz, S - 1), sz)
    for k in range(S):
        here = layer(post_ref, k)
        behind = layer(post_ref, max(k - 1, 0))
        ahead = layer(post_ref, min(k + 1, S - 1))
        moved = jnp.where(g.plus[0], behind, jnp.where(g.minus[0], ahead, here))
        moved = g.row_roll(g.row_roll(moved, 1, S), 2, 1)
        one_y, one_z, one_x, two, _ = g.crossings(k)
        out = jnp.where(one_y, lane_roll(sy, -S * k), moved)
        out = jnp.where(one_z, lane_roll(sz, -k), out)
        if one_x is not None:
            out = jnp.where(one_x, sx, out)
        out = jnp.where(two, g.opposite(here), out)
        store(k, out)


def stream_back(g, bar_ref, recv_ref, slots, tmp_ref, work_ref, out_ref):
    ox, oy, oz = received(g, recv_ref, slots, FACED, g.plus, tmp_ref)
    oy = jnp.where(g.plus[1], lane_roll(oy, -S), oy)
    oz = jnp.where(g.plus[2], lane_roll(oz, S - 1), oz)
    for k in range(S):
        put(work_ref, k, jnp.where(g.crossings(k)[4], layer(bar_ref, k), 0.0))
    for k in range(S):
        zero = jnp.zeros((R, A), F32)
        ahead = layer(work_ref, k + 1) if k + 1 < S else zero
        behind = layer(work_ref, k - 1) if k > 0 else zero
        moved = jnp.where(g.plus[0], ahead, jnp.where(g.minus[0], behind, layer(work_ref, k)))
        out = g.row_roll(g.row_roll(moved, 1, S, -1), 2, 1, -1)
        out += g.opposite(jnp.where(g.crossings(k)[3], layer(bar_ref, k), 0.0))
        out += jnp.where(g.oy, lane_roll(oy, -S * k), 0.0)
        out += jnp.where(g.oz, lane_roll(oz, -k), 0.0)
        if k == 0:
            out += jnp.where(g.minus[0], ox, 0.0)
        if k == S - 1:
            out += jnp.where(g.plus[0], ox, 0.0)
        put(out_ref, k, out)


def mm(a, b):
    return jnp.dot(a, b, preferred_element_type=F32)


def outer(a, b):
    return lax.dot_general(a, b, (((1,), (1,)), ((), ())), preferred_element_type=F32)


def slope(h):
    wide = h.astype(F32)
    return 1.0 - wide * wide


def collide(x, w_in, w_mid, w_out):
    inputs = x.astype(BF16)
    h0 = jnp.tanh(mm(w_in[...], inputs)).astype(BF16)
    h1 = jnp.tanh(mm(w_mid[...], h0)).astype(BF16)
    return inputs, h0, h1, x + mm(w_out[...], h1)


def collide_back(bar, inputs, h0, h1, w_in_t, w_mid_t, w_out_t, grads_ref, hid):
    e = bar.astype(BF16)
    a1 = (mm(w_out_t[...], e) * slope(h1)).astype(BF16)
    a0 = (mm(w_mid_t[...], a1) * slope(h0)).astype(BF16)
    grads_ref[:hid] += outer(a1, h0)
    grads_ref[hid : hid + R] += outer(inputs, a0)
    grads_ref[hid + R : hid + 2 * R] += outer(e, h1)
    return bar + mm(w_in_t[...], a0)


def span(i):
    return pl.ds(pl.multiple_of(i * CHUNK, CHUNK), CHUNK)


LANES = 128


def load_rows(dst, src):
    lines = dst.shape[1] // LANES
    dst[16:] = jnp.zeros((R - 16, dst.shape[1]), F32)
    for i in range(lines):
        dst[:Q, i * LANES : (i + 1) * LANES] = src[pl.ds(i, Q, stride=lines), :]


def store_lines(dst, first, value):
    lines = dst.shape[0] // Q
    for i in range(value.shape[1] // LANES):
        dst[pl.ds(first + i, Q, stride=lines), :] = value[:Q, i * LANES : (i + 1) * LANES]


def one_hot_layers(level, quadrant, pick):
    half = S // 2
    target = lax.broadcasted_iota(jnp.int32, (A, A), 1)
    source = lax.broadcasted_iota(jnp.int32, (A, A), 0)
    row, col = target // S, target % S
    fine = row // 2 * S + col // 2
    for face in range(6):
        q = quadrant[0, 0, face]
        high, low = q // 2, q % 2
        if face >= 4:
            high, low = low, high
        corner = high * half * S + low * half
        wanted = jnp.where(level[0, 0, face] == 1, corner + fine, target)
        pick[face] = jnp.where(source == wanted, 1.0, 0.0).astype(BF16)


def padded_rows(src, tall, flat, flipped):
    tall[...] = jnp.zeros(tall.shape, F32)
    tall[:Q] = src[...].astype(F32)
    flat[...] = tall[...].astype(BF16)
    flipped[...] = tall[...].T.astype(BF16)


def first_kernel(
    level, quadrant, table, pops, cot, w_in_rows, w_mid, w_out_rows,
    post, h_hbm, sheets, pick, w_in, w_in_t, w_out, w_out_t, w_mid_t, wide, cot_wide, h_buf, tall, sems,
):
    g = Geometry(table)
    cells = wide.shape[1]
    load_rows(wide, pops)
    load_rows(cot_wide, cot)
    padded_rows(w_in_rows, tall, w_in_t, w_in)
    padded_rows(w_out_rows, tall, w_out, w_out_t)
    w_mid_t[...] = w_mid[...].astype(F32).T.astype(BF16)
    one_hot_layers(level, quadrant, pick)
    sheets[...] = jnp.zeros(sheets.shape, F32)

    def moved(i, j):
        return pltpu.make_async_copy(h_buf.at[j, :, span(i)], h_hbm.at[j, :, span(i)], sems.at[j, i])

    @pl.loop(0, cells // CHUNK)
    def _(i):
        at = span(i)
        _, h0, h1, out = collide(wide[:, at], w_in, w_mid, w_out)
        post[:, at] = out
        h_buf[0, :, at] = h0
        h_buf[1, :, at] = h1
        moved(i, 0).start()
        moved(i, 1).start()

    gather_sheets(g, post, sheets)
    gather_bars(g, cot_wide, pick, sheets)

    @pl.loop(0, cells // CHUNK)
    def _(i):
        moved(i, 0).wait()
        moved(i, 1).wait()


def middle_kernel(
    blocks, source, table, pick, recv, post1, cot, w_in, w_mid, w_out, w_in_t, w_mid_t, w_out_t,
    post2, bar, sheets, grads, state, wide, work, pbar, tmp,
):
    g = Geometry(table)
    cells = post1.shape[1]
    hid = w_mid.shape[0]
    slots = [slot_of(source, blocks, face) for face in (0, 1)]
    load_rows(wide, cot)
    stream(g, post1, recv, slots, pick, tmp, functools.partial(put, state))
    stream_back(g, wide, recv, slots, tmp, work, pbar)
    grads[...] = jnp.zeros(grads.shape, F32)
    sheets[...] = jnp.zeros(sheets.shape, F32)

    @pl.loop(0, cells // CHUNK)
    def _(i):
        at = span(i)
        inputs, h0, h1, out = collide(state[:, at], w_in, w_mid, w_out)
        post2[:, at] = out
        bar[:, at] = collide_back(pbar[:, at], inputs, h0, h1, w_in_t, w_mid_t, w_out_t, grads, hid)

    gather_sheets(g, post2, sheets)
    gather_bars(g, bar, pick, sheets)


def last_kernel(
    blocks, source, table, pick, recv, post2, bar, pops, h_hbm, grads_in, w_in_t, w_mid_t, w_out_t,
    final, grad_pops, grads, wide, work, pbar, tmp, h_buf, sems,
):
    g = Geometry(table)
    cells = post2.shape[1]
    hid = w_mid_t.shape[0]

    def moved(i, j):
        return pltpu.make_async_copy(h_hbm.at[j, :, span(i)], h_buf.at[j, :, span(i)], sems.at[j, i])

    @pl.loop(0, cells // CHUNK)
    def _(i):
        moved(i, 0).start()
        moved(i, 1).start()

    slots = [slot_of(source, blocks, face) for face in (0, 1)]
    load_rows(wide, pops)
    stream(g, post2, recv, slots, pick, tmp, lambda k, value: store_lines(final, k * A // LANES, value))
    stream_back(g, bar, recv, slots, tmp, work, pbar)
    grads[...] = grads_in[...]

    @pl.loop(0, cells // CHUNK)
    def _(i):
        at = span(i)
        moved(i, 0).wait()
        moved(i, 1).wait()
        out = collide_back(
            pbar[:, at], wide[:, at].astype(BF16), h_buf[0, :, at], h_buf[1, :, at],
            w_in_t, w_mid_t, w_out_t, grads, hid,
        )
        pbar[:, at] = out

    store_lines(grad_pops, 0, pbar[...])


OFFSETS = [d for d in range(-REACH, REACH + 1) if d != 0]


def exchange_kernel(blocks, slabs, sheets, recv, send_sem, recv_sem):
    me, level = lax.axis_index("blocks"), lax.axis_index("slab")
    side = [lax.rem(me - d + blocks, blocks) for d in OFFSETS]
    other = me + 1 - 2 * lax.rem(me, 2)
    above, below = lax.rem(level + 1, slabs), lax.rem(level + slabs - 1, slabs)
    barrier = pltpu.get_barrier_semaphore()
    for target in side:
        pl.semaphore_signal(barrier, inc=1, device_id={"blocks": target}, device_id_type=MESH)
    for target in (above, below):
        pl.semaphore_signal(barrier, inc=1, device_id={"slab": target}, device_id_type=MESH)
    pl.semaphore_wait(barrier, len(side) + 2)
    plan = [(0, i, {"blocks": target}) for i, target in enumerate(side)]
    plan.append((1, len(side), {"blocks": other}))
    plan.append((2, len(side) + 1, {"slab": below}))
    plan.append((2, len(side) + 2, {"slab": above}))
    copies = []
    for which, slot, device in plan:
        copy = pltpu.make_async_remote_copy(
            src_ref=sheets.at[which], dst_ref=recv.at[slot],
            send_sem=send_sem.at[slot], recv_sem=recv_sem.at[slot],
            device_id=device, device_id_type=MESH,
        )
        copy.start()
        copies.append(copy)
    for copy in copies:
        copy.wait()


PIECES = 3


def sum_kernel(chips, slabs, grads, out, land_c, half, land_t, part, land_s, sems):
    me, level = lax.axis_index("blocks"), lax.axis_index("slab")
    core, chip = lax.rem(me, 2), me // 2
    rows, width = part.shape[1], land_s.shape[-1]
    peer_t = [lax.rem(chip + d, chips) for d in range(1, chips)]
    peer_s = [lax.rem(level + d, slabs) for d in range(1, slabs)]
    twin = {"blocks": me + 1 - 2 * core}
    sides = [{"blocks": 2 * t + core} for t in peer_t]
    stack = [{"slab": t} for t in peer_s]
    barrier = pltpu.get_barrier_semaphore()
    for device in [twin] + sides + stack:
        pl.semaphore_signal(barrier, inc=1, device_id=device, device_id_type=MESH)
    pl.semaphore_wait(barrier, 1 + len(sides) + len(stack))

    def send(src, dst, p, which, device):
        copy = pltpu.make_async_remote_copy(
            src_ref=src, dst_ref=dst, send_sem=sems.at[0, p, which], recv_sem=sems.at[1, p, which],
            device_id=device, device_id_type=MESH,
        )
        copy.start()
        return copy

    def half_of(p, c):
        return pl.ds(pl.multiple_of((2 * p + c) * chips * rows, 8), chips * rows)

    def row_of(p):
        return pl.ds(pl.multiple_of(((2 * p + core) * chips + chip) * rows, 8), rows)

    def lane_of(i):
        return pl.ds(pl.multiple_of(i * width, 128), width)

    first_t, first_s = 1, len(sides) + 1
    again = len(sides) + len(stack) + 1
    flying = [[] for _ in range(PIECES)]
    sent = []

    def stage(p, number):
        for copy in flying[p]:
            copy.wait_recv()
        sent.extend(flying[p])
        flying[p] = []
        if number == 0:
            flying[p] = [send(grads.at[half_of(p, 1 - core)], land_c.at[p], p, 0, twin)]
        if number == 1:
            half[p] = grads[half_of(p, core)] + land_c[p]
            flying[p] = [
                send(half.at[p, pl.ds(pl.multiple_of(t * rows, 8), rows)], land_t.at[p, i], p, first_t + i, device)
                for i, (t, device) in enumerate(zip(peer_t, sides))
            ]
        if number == 2:
            total = half[p, pl.ds(pl.multiple_of(chip * rows, 8), rows)]
            for i in range(len(sides)):
                total += land_t[p, i]
            part[p] = total
            flying[p] = [
                send(part.at[p, :, lane_of(t)], land_s.at[p, i], p, first_s + i, device)
                for i, (t, device) in enumerate(zip(peer_s, stack))
            ]
        if number == 3:
            mine = part[p, :, lane_of(level)]
            for i in range(len(stack)):
                mine += land_s[p, i]
            out[row_of(p), lane_of(level)] = mine
            spot = out.at[row_of(p), lane_of(level)]
            flying[p] = [send(spot, spot, p, again + first_s + i, device) for i, device in enumerate(stack)]
        if number == 4:
            spot = out.at[row_of(p)]
            flying[p] = [send(spot, spot, p, again + first_t + i, device) for i, device in enumerate(sides)]
        if number == 5:
            spot = out.at[half_of(p, core)]
            flying[p] = [send(spot, spot, p, again, twin)]

    for number in (0, 1):
        for p in range(PIECES):
            stage(p, number)
    for tick in range(2, 5 + PIECES + 2):
        for p in range(PIECES):
            number = tick - p
            if 2 <= number <= 6:
                stage(p, number)
    for copy in sent:
        copy.wait_send()


def vmem(count):
    return [pl.BlockSpec(memory_space=pltpu.VMEM)] * count


SMEM_SPEC = pl.BlockSpec(memory_space=pltpu.SMEM)
ANY_SPEC = pl.BlockSpec(memory_space=pl.ANY)
LIMIT = 60 * 1024 * 1024


def shape(dims, dtype=F32):
    return jax.ShapeDtypeStruct(dims, dtype)


def shards(blocks, slabs, populations, w_in, w_mid, w_out, cotangent, face_source, face_level, face_quadrant):
    cells = populations.shape[-1]
    hid = w_in.shape[0]
    pops, cot = (v.reshape(Q * cells // LANES, LANES) for v in (populations, cotangent))
    table = jnp.asarray(row_table())
    w_mid = w_mid[0]
    step = 8 * blocks * PIECES
    total_rows = -(-(hid + 2 * R) // step) * step
    parts = cells // CHUNK
    volume = pltpu.VMEM((R, cells), F32)
    tmp = pltpu.VMEM((R, A), F32)
    sheet_rows = 24
    params = pltpu.CompilerParams(vmem_limit_bytes=LIMIT)

    def exchange(sheets, which):
        count = 2 * REACH + 3
        return pl.pallas_call(
            functools.partial(exchange_kernel, blocks, slabs),
            out_shape=shape((count, sheet_rows, A)),
            in_specs=vmem(1),
            out_specs=vmem(1)[0],
            scratch_shapes=[pltpu.SemaphoreType.DMA((count,)), pltpu.SemaphoreType.DMA((count,))],
            compiler_params=pltpu.CompilerParams(collective_id=which, has_side_effects=True),
            name=f"exchange{which}",
        )(sheets)

    post1, hidden, sheets, pick, w_in, w_in_t, w_out, w_out_t, w_mid_t = pl.pallas_call(
        first_kernel,
        out_shape=(
            shape((R, cells)), shape((2, hid, cells), BF16), shape((3, sheet_rows, A)), shape((6, A, A), BF16),
            shape((hid, R), BF16), shape((R, hid), BF16), shape((R, hid), BF16), shape((hid, R), BF16),
            shape((hid, hid), BF16),
        ),
        in_specs=[SMEM_SPEC] * 2 + vmem(6),
        out_specs=(vmem(1)[0], ANY_SPEC, *vmem(7)),
        scratch_shapes=[
            volume, volume, pltpu.VMEM((2, hid, cells), BF16), pltpu.VMEM((R, hid), F32),
            pltpu.SemaphoreType.DMA((2, parts)),
        ],
        compiler_params=params,
        name="first",
    )(face_level, face_quadrant, table, pops, cot, w_in.T, w_mid, w_out)
    backs = (w_in_t, w_mid_t, w_out_t)
    recv = exchange(sheets, 0)
    post2, bar, sheets, grads = pl.pallas_call(
        functools.partial(middle_kernel, blocks),
        out_shape=(shape((R, cells)), shape((R, cells)), shape((3, sheet_rows, A)), shape((total_rows, hid))),
        in_specs=[SMEM_SPEC] + vmem(11),
        out_specs=tuple(vmem(4)),
        scratch_shapes=[volume] * 4 + [tmp],
        compiler_params=params,
        name="middle",
    )(face_source.T, table, pick, recv, post1, cot, w_in, w_mid, w_out, *backs)
    recv = exchange(sheets, 1)
    final, grad_pops, grads = pl.pallas_call(
        functools.partial(last_kernel, blocks),
        out_shape=(shape(pops.shape), shape(pops.shape), shape((total_rows, hid))),
        in_specs=[SMEM_SPEC] + vmem(6) + [ANY_SPEC] + vmem(4),
        out_specs=tuple(vmem(3)),
        scratch_shapes=[volume] * 3 + [tmp, pltpu.VMEM((2, hid, cells), BF16), pltpu.SemaphoreType.DMA((2, parts))],
        compiler_params=params,
        name="last",
    )(face_source.T, table, pick, recv, post2, bar, pops, hidden, grads, *backs)
    chips = blocks // 2
    rows, width = total_rows // (blocks * PIECES), hid // slabs
    total = pl.pallas_call(
        functools.partial(sum_kernel, chips, slabs),
        out_shape=shape((total_rows, hid)),
        in_specs=vmem(1),
        out_specs=vmem(1)[0],
        scratch_shapes=[
            pltpu.VMEM((PIECES, chips * rows, hid), F32),
            pltpu.VMEM((PIECES, chips * rows, hid), F32),
            pltpu.VMEM((PIECES, chips - 1, rows, hid), F32),
            pltpu.VMEM((PIECES, rows, hid), F32),
            pltpu.VMEM((PIECES, slabs - 1, rows, width), F32),
            pltpu.SemaphoreType.DMA((2, PIECES, 2 * (chips + slabs - 1))),
        ],
        compiler_params=pltpu.CompilerParams(collective_id=2, has_side_effects=True),
        name="sum_all",
    )(grads)
    total = total * float(blocks * slabs * cells) ** (-0.5)
    return (
        final.reshape(populations.shape),
        grad_pops.reshape(populations.shape),
        total[hid : hid + Q].T,
        total[:hid][None],
        total[hid + R : hid + R + Q],
    )


def solution(mesh):
    spread = P(None, "slab", "blocks", None)
    in_specs = (spread, P(), P(), P(), spread, P(), P("slab", "blocks", None), P("slab", "blocks", None))
    out_specs = (spread, spread, P(), P(), P())
    body = functools.partial(shards, mesh.shape["blocks"], mesh.shape["slab"])
    return jax.shard_map(body, mesh=mesh, in_specs=in_specs, out_specs=out_specs, check_vma=False)
```
